512 devices in a mesh: lat: 16 (over z, x_hi), lon: 32 (over y, x_lo, core).
Axes of the slice: x: 4 (x_hi: 2, x_lo: 2; x = x_hi * 2 + x_lo), y: 8, z: 8, core: 2. Of those that a mesh axis runs over, the one named last changes fastest.
Arguments:
- frame: bfloat16 [256, 512, 256], P('lat', 'lon'), may hold values from -64 to 64
- weight_qkv: bfloat16 [256, 768], replicated, may hold values from -0.375 to 0.375
- weight_proj: bfloat16 [256, 256], replicated, may hold values from -0.375 to 0.375
- gain_attn: float32 [256], replicated, may hold values from 0.5 to 1.5
- weight_up: bfloat16 [256, 1024], replicated, may hold values from -0.375 to 0.375
- weight_down: bfloat16 [1024, 256], replicated, may hold values from -0.1875 to 0.1875
- gain_mlp: float32 [256], replicated, may hold values from 0.5 to 1.5
- cotangent: bfloat16 [256, 512, 256], P('lat', 'lon'), may hold values from -6 to 6
Outputs:
- block_out: bfloat16 [256, 512, 256], P('lat', 'lon')
- grad_frame: bfloat16 [256, 512, 256], P('lat', 'lon')
- grad_qkv: bfloat16 [256, 768], replicated
- grad_proj: bfloat16 [256, 256], replicated
- grad_up: bfloat16 [256, 1024], replicated
- grad_down: bfloat16 [1024, 256], replicated
- grad_gain_attn: float32 [256], replicated
- grad_gain_mlp: float32 [256], replicated
The draws below stay inside these ranges and needn't reach their ends.
All inputs are finite; a program needn't handle non-finite values.
Results may differ from the reference program's by a relative error of at most 0.012.
The reference program's roundings to bfloat16 on the way count: a program that leaves them out, or rounds other values in their place, can miss the bound.
Values may be sent and summed in bfloat16 or wider, within the bound.
No kernel may reach another device: no remote copies, remote signals or barrier semaphores. Data moves between devices by JAX's collectives and lax.ppermute only.
A program may use at most 128 MiB of HBM per device.

```python
import jax
import jax.numpy as jnp
from jax import lax

D = 256
HEADS = 8
FF = 1024
RADIUS = 6
HD = 32
LATS = 256
LONS = 512
TOKENS = 131072


def draw_frame(key, part):
    streams = jax.random.split(key, 3)
    channel_scale = jnp.exp(jax.random.uniform(streams[0], (D,), jnp.float32, -0.5, 0.5))
    base = jax.random.normal(streams[2], (LATS, LONS, D), jnp.float32) * channel_scale
    return jnp.clip(base, -10.0, 10.0).astype(jnp.bfloat16)


def shard_levels(key, dims, cuts, least, largest):
    gain = 1.0
    for axis_at, blocks in cuts:
        draws = jax.random.uniform(jax.random.fold_in(jax.random.fold_in(key, 6), axis_at), (blocks,), jnp.float32, least / len(cuts), largest / len(cuts))
        gain = gain * jnp.repeat(jnp.exp(draws), dims[axis_at] // blocks).reshape((-1,) + (1,) * (len(dims) - 1 - axis_at))
    return gain


def scatter_about(own_key, extent, scale, limit, shards=(), kind=jnp.bfloat16):
    values = scale * jax.random.normal(own_key, extent, jnp.float32)
    if shards:
        values = values * shard_levels(own_key, extent, shards, -0.22, 0.18)
    return jnp.clip(values, -limit, limit).astype(kind)


def setup_inputs(seed: int = 0) -> dict:
    seeds = jax.random.split(jax.random.key(seed), 9)
    frame = draw_frame(jax.random.fold_in(seeds[8], 71), 0)
    weight_qkv = scatter_about(seeds[1], (D, 3 * D), D ** -0.5, 0.375)
    weight_proj = scatter_about(seeds[2], (D, D), D ** -0.5, 0.375)
    gain_attn = jnp.clip(1.0 + 0.1 * jax.random.normal(seeds[3], (D,), jnp.float32), 0.5, 1.5)
    weight_up = scatter_about(seeds[4], (D, FF), D ** -0.5, 0.375)
    weight_down = scatter_about(seeds[5], (FF, D), FF ** -0.5, 0.1875)
    gain_mlp = jnp.clip(1.0 + 0.1 * jax.random.normal(seeds[6], (D,), jnp.float32), 0.5, 1.5)
    cotangent = scatter_about(seeds[7], (LATS, LONS, D), 1.0, 6.0, ((0, 16), (1, 32)))
    return {"frame": frame, "weight_qkv": weight_qkv, "weight_proj": weight_proj, "gain_attn": gain_attn, "weight_up": weight_up, "weight_down": weight_down, "gain_mlp": gain_mlp, "cotangent": cotangent}


epsilon = 1e-06
cubic_term = 0.044715
gelu_root = 0.7978845608028654
negative_big = -1e+30

def gelu_pair(upward):
    tangent = jnp.tanh(gelu_root * (upward + cubic_term * upward * upward * upward))
    activated = 0.5 * upward * (1.0 + tangent)
    derivative = 0.5 * (1.0 + tangent) + 0.5 * upward * (1.0 - tangent * tangent) * gelu_root * (1.0 + 3.0 * cubic_term * upward * upward)
    return (activated, derivative)

def rms_factor(field):
    return lax.rsqrt(lax.optimization_barrier(jnp.mean(field * field, axis=-1, keepdims=True)) + epsilon)

def norm_backward(incoming, field, factor):
    mean_term = lax.optimization_barrier(jnp.mean(incoming * field, axis=-1, keepdims=True))
    return factor * (incoming - field * factor * factor * mean_term)

def pad_grid(field):
    wrapped = jnp.pad(field, ((0, 0), (RADIUS, RADIUS), (0, 0), (0, 0)), mode='wrap')
    return jnp.pad(wrapped, ((RADIUS, RADIUS), (0, 0), (0, 0), (0, 0)))

def window_start(offset):
    span = 2 * RADIUS + 1
    zero = jnp.zeros((), jnp.int32)
    return ((offset // span).astype(jnp.int32), (offset % span).astype(jnp.int32), zero, zero)

def shifted(padded, offset):
    return lax.dynamic_slice(padded, window_start(offset), (LATS, LONS, HEADS, HD))

def add_window(padded, contribution, offset):
    return lax.dynamic_update_slice(padded, shifted(padded, offset) + contribution, window_start(offset))

def rows_valid(offset):
    span = 2 * RADIUS + 1
    rows = jnp.arange(LATS, dtype=jnp.int32) + (offset // span).astype(jnp.int32) - RADIUS
    return ((rows >= 0) & (rows < LATS))[:, None, None]

def fold_longitude(padded):
    core = padded[RADIUS:RADIUS + LATS]
    middle = core[:, RADIUS:RADIUS + LONS]
    front = jnp.pad(core[:, :RADIUS], ((0, 0), (LONS - RADIUS, 0), (0, 0), (0, 0)))
    back = jnp.pad(core[:, LONS + RADIUS:], ((0, 0), (0, LONS - RADIUS), (0, 0), (0, 0)))
    return middle + front + back

def reference(frame, weight_qkv, weight_proj, gain_attn, weight_up, weight_down, gain_mlp, cotangent):
    head_scale = HD ** (-0.5)
    grad_scale = TOKENS ** (-0.5)
    span = 2 * RADIUS + 1
    offsets = jnp.arange(span * span, dtype=jnp.int32)
    flat = frame.reshape(TOKENS, D)
    projected = jnp.dot(flat, weight_qkv, preferred_element_type=jnp.float32).astype(jnp.bfloat16)
    queries32 = projected[:, :D].reshape(LATS, LONS, HEADS, HD).astype(jnp.float32)
    keys_pad = pad_grid(projected[:, D:2 * D].reshape(LATS, LONS, HEADS, HD))
    values_pad = pad_grid(projected[:, 2 * D:].reshape(LATS, LONS, HEADS, HD))

    def score_one(offset):
        raw = lax.optimization_barrier(jnp.sum(queries32 * shifted(keys_pad, offset).astype(jnp.float32), axis=-1)) * head_scale
        return jnp.where(rows_valid(offset), raw, negative_big)
    scores = lax.map(score_one, offsets)
    peak = lax.optimization_barrier(jnp.max(scores, axis=0, keepdims=True))
    expo = jnp.exp(scores - peak)
    probs = expo / lax.optimization_barrier(jnp.sum(expo, axis=0, keepdims=True))
    probs_bf = probs.astype(jnp.bfloat16)

    def attend_step(carry, offset):
        weight = probs_bf[offset].astype(jnp.float32)[..., None]
        return (carry + weight * shifted(values_pad, offset).astype(jnp.float32), None)
    start_sum = jnp.zeros((LATS, LONS, HEADS, HD), jnp.float32)
    attended = lax.scan(attend_step, start_sum, offsets)[0].astype(jnp.bfloat16).reshape(TOKENS, D)
    proj = jnp.dot(attended, weight_proj, preferred_element_type=jnp.float32)
    factor_one = rms_factor(proj)
    mid = (flat.astype(jnp.float32) + proj * factor_one * gain_attn).astype(jnp.bfloat16)
    upward = jnp.dot(mid, weight_up, preferred_element_type=jnp.float32)
    activated, derivative = gelu_pair(upward)
    hidden = activated.astype(jnp.bfloat16)
    downward = jnp.dot(hidden, weight_down, preferred_element_type=jnp.float32)
    factor_two = rms_factor(downward)
    block_out = (mid.astype(jnp.float32) + downward * factor_two * gain_mlp).astype(jnp.bfloat16)
    incoming = cotangent.reshape(TOKENS, D).astype(jnp.float32)
    grad_gain_mlp = lax.optimization_barrier(jnp.sum(incoming * downward * factor_two, axis=0)) * grad_scale
    d_down = norm_backward(incoming * gain_mlp, downward, factor_two).astype(jnp.bfloat16)
    grad_down = (jnp.dot(hidden.T, d_down, preferred_element_type=jnp.float32) * grad_scale).astype(jnp.bfloat16)
    d_up = (jnp.dot(d_down, weight_down.T, preferred_element_type=jnp.float32) * derivative).astype(jnp.bfloat16)
    grad_up = (jnp.dot(mid.T, d_up, preferred_element_type=jnp.float32) * grad_scale).astype(jnp.bfloat16)
    d_mid = incoming + jnp.dot(d_up, weight_up.T, preferred_element_type=jnp.float32)
    grad_gain_attn = lax.optimization_barrier(jnp.sum(d_mid * proj * factor_one, axis=0)) * grad_scale
    d_proj = norm_backward(d_mid * gain_attn, proj, factor_one).astype(jnp.bfloat16)
    grad_proj = (jnp.dot(attended.T, d_proj, preferred_element_type=jnp.float32) * grad_scale).astype(jnp.bfloat16)
    d_attended = jnp.dot(d_proj, weight_proj.T, preferred_element_type=jnp.float32).astype(jnp.bfloat16)
    d_attended32 = d_attended.reshape(LATS, LONS, HEADS, HD).astype(jnp.float32)

    def probe_one(offset):
        return lax.optimization_barrier(jnp.sum(d_attended32 * shifted(values_pad, offset).astype(jnp.float32), axis=-1))
    d_probs = lax.map(probe_one, offsets)
    d_weighted = lax.optimization_barrier(jnp.sum(probs * d_probs, axis=0, keepdims=True))
    d_scores = (probs * (d_probs - d_weighted) * head_scale).astype(jnp.bfloat16)

    def gather_step(carry, offset):
        query_sum, key_sum, value_sum = carry
        score_weight = d_scores[offset].astype(jnp.float32)[..., None]
        prob_weight = probs_bf[offset].astype(jnp.float32)[..., None]
        query_sum = query_sum + score_weight * shifted(keys_pad, offset).astype(jnp.float32)
        key_sum = add_window(key_sum, score_weight * queries32, offset)
        value_sum = add_window(value_sum, prob_weight * d_attended32, offset)
        return ((query_sum, key_sum, value_sum), None)
    pad_zero = jnp.zeros((LATS + 2 * RADIUS, LONS + 2 * RADIUS, HEADS, HD), jnp.float32)
    sums = lax.scan(gather_step, (start_sum, pad_zero, pad_zero), offsets)[0]
    d_projected = jnp.concatenate([sums[0].reshape(TOKENS, D), fold_longitude(sums[1]).reshape(TOKENS, D), fold_longitude(sums[2]).reshape(TOKENS, D)], axis=1).astype(jnp.bfloat16)
    grad_qkv = (jnp.dot(flat.T, d_projected, preferred_element_type=jnp.float32) * grad_scale).astype(jnp.bfloat16)
    grad_frame = (d_mid + jnp.dot(d_projected, weight_qkv.T, preferred_element_type=jnp.float32)).astype(jnp.bfloat16)
    return (block_out.reshape(LATS, LONS, D), grad_frame.reshape(LATS, LONS, D), grad_qkv, grad_proj, grad_up, grad_down, grad_gain_attn, grad_gain_mlp)
```

```python
import functools

import jax
import jax.numpy as jnp
from jax import lax
from jax.experimental import pallas as pl
from jax.experimental.pallas import tpu as pltpu
from jax.sharding import PartitionSpec as P

HEADS = 8
RADIUS = 6
EDGE = 8

epsilon = 1e-06
cubic_term = 0.044715
gelu_root = 0.7978845608028654
negative_big = -1e30

F32 = jnp.float32
BF16 = jnp.bfloat16


def nn(left, right):
    return lax.dot_general(left, right, (((1,), (0,)), ((), ())), preferred_element_type=F32)


def nt(left, right):
    return lax.dot_general(left, right, (((1,), (1,)), ((), ())), preferred_element_type=F32)


def gelu_pair(upward):
    tangent = jnp.tanh(gelu_root * (upward + cubic_term * upward * upward * upward))
    activated = 0.5 * upward * (1.0 + tangent)
    derivative = 0.5 * (1.0 + tangent) + 0.5 * upward * (1.0 - tangent * tangent) * gelu_root * (
        1.0 + 3.0 * cubic_term * upward * upward
    )
    return (activated, derivative)


def rms_factor(field):
    return lax.rsqrt(jnp.mean(field * field, axis=-1, keepdims=True) + epsilon)


def norm_backward(incoming, field, factor):
    mean_term = jnp.mean(incoming * field, axis=-1, keepdims=True)
    return factor * (incoming - field * factor * factor * mean_term)


def local_kernel(
    dims,
    where_ref,
    frame_ref,
    wide_ref,
    top_ref,
    bottom_ref,
    wqkv_ref,
    wproj_ref,
    gain_attn_ref,
    wup_ref,
    wdown_ref,
    gain_mlp_ref,
    cot_ref,
    block_out_ref,
    d_mid_ref,
    dq_ref,
    up_ref,
    down_ref,
    centre_ref,
    grads_ref,
    gains_ref,
    halo,
    keys,
    values,
    keys_t,
    values_t,
    stack_q,
    stack_o,
    bias,
    probs,
    probs_bf,
    d_scores,
    att_t,
    dq_t,
    hidden,
    slope,
    pair_grads,
):
    rows, cols, lat_total = dims["rows"], dims["cols"], dims["lat_total"]
    heads, size, width, ff = HEADS, dims["width"] // HEADS, dims["width"], dims["ff"]
    across = cols + 2 * EDGE
    block_rows = 128 // cols
    blocks = rows // block_rows
    reach = (block_rows + 2 * RADIUS) * across
    step = block_rows * across
    pairs = heads // 2
    head_scale = size ** (-0.5)
    lat_first = where_ref[0]
    core = where_ref[1]
    side = (core, 1 - core)

    def put(index, value):
        half, row = divmod(index, 6)
        grads_ref[side[half], row * 512 : row * 512 + 256, :] = value[:, :128]
        grads_ref[side[half], row * 512 + 256 : row * 512 + 512, :] = value[:, 128:]

    rim = RADIUS * across
    inner = rows * across
    halo[0:rim, :] = top_ref[...]
    halo[rim : rim + inner, :] = wide_ref[...]
    halo[rim + inner : inner + 2 * rim, :] = bottom_ref[...]
    grid = halo[...]
    key32 = nn(grid, wqkv_ref[:, width : 2 * width])
    keys[...] = key32.astype(BF16)
    keys_t[...] = key32.T.astype(BF16)
    value32 = nn(grid, wqkv_ref[:, 2 * width :])
    values[...] = value32.astype(BF16)
    values_t[...] = value32.T.astype(BF16)

    lane_head = lax.broadcasted_iota(jnp.int32, (128, width), 1) // size

    def spread(target, field):
        for b in range(blocks):
            part = field[b * 128 : (b + 1) * 128]
            for h in range(heads):
                target[b, h * 128 : (h + 1) * 128, :] = jnp.where(lane_head == h, part, 0.0).astype(BF16)

    own = frame_ref[...]
    spread(stack_q, nn(own, wqkv_ref[:, :width]).astype(BF16).astype(F32))

    at_key = lax.broadcasted_iota(jnp.int32, (reach, 128), 0)
    at_query = lax.broadcasted_iota(jnp.int32, (reach, 128), 1)
    key_row, key_col = at_key // across, at_key % across
    key_col = jnp.where(key_col < cols + EDGE, key_col, key_col - across)
    row_gap = key_row - at_query // cols
    col_gap = key_col - at_query % cols
    near = (row_gap >= 0) & (row_gap <= 2 * RADIUS) & (col_gap >= -RADIUS) & (col_gap <= RADIUS)
    for b in range(blocks):
        row_global = key_row + (lat_first + b * block_rows - RADIUS)
        seen = near & (row_global >= 0) & (row_global < lat_total)
        bias[b] = jnp.where(seen, 0.0, negative_big)

    def diagonal(target, product, b, pair):
        at = pl.multiple_of(pair * 2 * size, 2 * size)
        lane = pl.multiple_of(b * 128, 128)
        target[pl.ds(at, size), pl.ds(lane, 128)] = product[:size, :128]
        target[pl.ds(at + size, size), pl.ds(lane, 128)] = product[size:, 128:]

    def forward(index, _):
        b, pair = index // pairs, index % pairs
        at = pl.multiple_of(pair * 256, 256)
        first = pl.multiple_of(b * step, step)
        rim_bias = bias[b]
        scores = nt(keys[pl.ds(first, reach), :], stack_q[b, pl.ds(at, 256), :]) * head_scale
        scores = scores + jnp.concatenate([rim_bias, rim_bias], axis=1)
        peak = jnp.max(scores, axis=0, keepdims=True)
        expo = jnp.exp(scores - peak)
        total = jnp.sum(expo, axis=0, keepdims=True)
        weight = expo * (1.0 / total)
        probs[index] = weight
        weight_bf = weight.astype(BF16)
        probs_bf[b, :, pl.ds(at, 256)] = weight_bf
        some = values_t[pl.ds(pl.multiple_of(pair * 2 * size, 2 * size), 2 * size), pl.ds(first, reach)]
        diagonal(att_t, nn(some, weight_bf), b, pair)
        return _

    lax.fori_loop(0, blocks * pairs, forward, 0)

    attended_t = att_t[...]
    attended = attended_t.T.astype(BF16)
    proj = nn(attended, wproj_ref[...])
    factor_one = rms_factor(proj)
    mid32 = own.astype(F32) + proj * factor_one * gain_attn_ref[...]
    mid = mid32.astype(BF16)

    downward = jnp.zeros((rows * cols, width), F32)
    for c in range(ff // 256):
        upward = nn(mid, wup_ref[:, c * 256 : (c + 1) * 256])
        activated, derivative = gelu_pair(upward)
        hidden_c = activated.astype(BF16)
        hidden[c] = activated
        slope[c] = derivative
        downward = downward + nn(hidden_c, wdown_ref[c * 256 : (c + 1) * 256, :])
    factor_two = rms_factor(downward)
    block_out_ref[...] = (mid.astype(F32) + downward * factor_two * gain_mlp_ref[...]).astype(BF16)

    incoming = cot_ref[...].astype(F32)
    gain_term = incoming * downward * factor_two
    gains_ref[side[1]] = jnp.broadcast_to(jnp.sum(gain_term.T, axis=1, keepdims=True), (width, 128))
    d_down = norm_backward(incoming * gain_mlp_ref[...], downward, factor_two).astype(BF16)
    mid_t = mid.astype(F32).T.astype(BF16)
    d_mid = incoming
    for c in range(ff // 256):
        d_up = (nt(d_down, wdown_ref[c * 256 : (c + 1) * 256, :]) * slope[c]).astype(BF16)
        d_mid = d_mid + nt(d_up, wup_ref[:, c * 256 : (c + 1) * 256])
        put(c, nn(mid_t, d_up))
        put(6 + c, nn(hidden[c].T.astype(BF16), d_down))
    d_mid_ref[...] = d_mid
    gain_term = d_mid * proj * factor_one
    gains_ref[side[0]] = jnp.broadcast_to(jnp.sum(gain_term.T, axis=1, keepdims=True), (width, 128))
    d_proj = norm_backward(d_mid * gain_attn_ref[...], proj, factor_one).astype(BF16)
    put(4, nn(attended_t.astype(BF16), d_proj))
    spread(stack_o, nt(d_proj, wproj_ref[...]).astype(BF16).astype(F32))

    def backward(index, _):
        b, pair = index // pairs, index % pairs
        at = pl.multiple_of(pair * 256, 256)
        first = pl.multiple_of(b * step, step)
        d_probs = nt(values[pl.ds(first, reach), :], stack_o[b, pl.ds(at, 256), :])
        weight = probs[index]
        d_weighted = jnp.sum(weight * d_probs, axis=0, keepdims=True)
        d_score = (weight * (d_probs - d_weighted) * head_scale).astype(BF16)
        d_scores[b, :, pl.ds(at, 256)] = d_score
        some = keys_t[pl.ds(pl.multiple_of(pair * 2 * size, 2 * size), 2 * size), pl.ds(first, reach)]
        diagonal(dq_t, nn(some, d_score), b, pair)
        return _

    lax.fori_loop(0, blocks * pairs, backward, 0)

    pair_grads[...] = jnp.zeros_like(pair_grads)
    for b in range(blocks):
        pair_grads[b * step : b * step + reach, :width] += nn(d_scores[b], stack_q[b])
        pair_grads[b * step : b * step + reach, width:] += nn(probs_bf[b], stack_o[b])

    dq = dq_t[...].T.astype(BF16)
    dq_ref[...] = dq
    up_ref[...] = pair_grads[0:rim, :].astype(BF16)
    down_ref[...] = pair_grads[rim + inner : inner + 2 * rim, :].astype(BF16)
    centre_ref[...] = pair_grads[rim : rim + inner, :]

    put(5, nn(own.astype(F32).T.astype(BF16), dq))
    grid_t = halo[...].astype(F32).T.astype(BF16)
    for half in range(2):
        terms = pair_grads[:, half * width : (half + 1) * width]
        high = terms.astype(BF16)
        low = (terms - high.astype(F32)).astype(BF16)
        put(10 + half, nn(grid_t, high) + nn(grid_t, low))


def local_part(where, frame, wide, top, bottom, weights, cotangent, dims):
    rows, cols, width, ff = dims["rows"], dims["cols"], dims["width"], dims["ff"]
    across = cols + 2 * EDGE
    grid = (rows + 2 * RADIUS) * across
    rim = RADIUS * across
    block_rows = 128 // cols
    blocks = rows // block_rows
    reach = (block_rows + 2 * RADIUS) * across
    tokens = rows * cols
    pairs = HEADS // 2
    shape = jax.ShapeDtypeStruct
    vmem = pl.BlockSpec(memory_space=pltpu.VMEM)
    outs = [
        shape((tokens, width), BF16),
        shape((tokens, width), F32),
        shape((tokens, width), BF16),
        shape((rim, 2 * width), BF16),
        shape((rim, 2 * width), BF16),
        shape((rows * across, 2 * width), F32),
        shape((2, 3072, 128), F32),
        shape((2, width, 128), F32),
    ]
    return pl.pallas_call(
        functools.partial(local_kernel, dims),
        out_shape=outs,
        in_specs=[pl.BlockSpec(memory_space=pltpu.SMEM)] + [vmem] * 11,
        out_specs=[vmem] * len(outs),
        scratch_shapes=[
            pltpu.VMEM((grid, width), BF16),
            pltpu.VMEM((grid, width), BF16),
            pltpu.VMEM((grid, width), BF16),
            pltpu.VMEM((width, grid), BF16),
            pltpu.VMEM((width, grid), BF16),
            pltpu.VMEM((blocks, HEADS * 128, width), BF16),
            pltpu.VMEM((blocks, HEADS * 128, width), BF16),
            pltpu.VMEM((blocks, reach, 128), F32),
            pltpu.VMEM((blocks * pairs, reach, 256), F32),
            pltpu.VMEM((blocks, reach, HEADS * 128), BF16),
            pltpu.VMEM((blocks, reach, HEADS * 128), BF16),
            pltpu.VMEM((width, tokens), F32),
            pltpu.VMEM((width, tokens), F32),
            pltpu.VMEM((ff // 256, tokens, 256), F32),
            pltpu.VMEM((ff // 256, tokens, 256), F32),
            pltpu.VMEM((grid, 2 * width), F32),
        ],
        name="local_part",
    )(where, frame, wide, top, bottom, *weights, cotangent)


def chip_groups(lat_n, lon_n):
    def flat(z, x, y, core):
        return (z * 2 + x // 2) * lon_n + y * 4 + x % 2 * 2 + core

    n_z, n_y = lat_n // 2, lon_n // 4
    over_x = [
        [flat(z, x, y, core) for x in range(4)] for z in range(n_z) for y in range(n_y) for core in range(2)
    ]
    over_yz = [
        [flat(z, x, y, core) for z in range(n_z) for y in range(n_y)] for x in range(4) for core in range(2)
    ]
    return over_x, over_yz


def on_device(
    frame, weight_qkv, weight_proj, gain_attn, weight_up, weight_down, gain_mlp, cotangent
):
    rows, cols, width = frame.shape
    ff = weight_up.shape[1]
    lat_n, lon_n = lax.axis_size("lat"), lax.axis_size("lon")
    tokens = rows * cols
    grad_scale = (tokens * lat_n * lon_n) ** (-0.5)
    across = cols + 2 * EDGE
    dims = {"rows": rows, "cols": cols, "width": width, "ff": ff, "lat_total": rows * lat_n}
    core = lax.axis_index("lon") % 2
    where = jnp.stack([lax.axis_index("lat") * rows, core]).astype(jnp.int32)

    east = [(i, (i + 1) % lon_n) for i in range(lon_n)]
    west = [(j, i) for i, j in east]
    south = [(i, i + 1) for i in range(lat_n - 1)]
    north = [(j, i) for i, j in south]

    from_east = lax.ppermute(frame[:, :EDGE], "lon", west)
    from_west = lax.ppermute(frame[:, cols - EDGE :], "lon", east)
    wide = jnp.concatenate([frame, from_east, from_west], axis=1)
    bottom = lax.ppermute(wide[:RADIUS], "lat", north)
    top = lax.ppermute(wide[rows - RADIUS :], "lat", south)

    weights = (
        weight_qkv,
        weight_proj,
        gain_attn.reshape(1, width),
        weight_up,
        weight_down,
        gain_mlp.reshape(1, width),
    )
    flat = (-1, width)
    block_out, d_mid, dq, up, down, centre, grads, gains = local_part(
        where,
        frame.reshape(flat),
        wide.reshape(flat),
        top.reshape(flat),
        bottom.reshape(flat),
        weights,
        cotangent.reshape(flat),
        dims,
    )

    up = lax.ppermute(up, "lat", north).reshape(RADIUS, across, 2 * width).astype(F32)
    down = lax.ppermute(down, "lat", south).reshape(RADIUS, across, 2 * width).astype(F32)
    rest = rows - RADIUS
    centre = centre.reshape(rows, across, 2 * width)
    centre = centre + jnp.pad(up, ((rest, 0), (0, 0), (0, 0))) + jnp.pad(down, ((0, rest), (0, 0), (0, 0)))
    to_east = centre[:, cols : cols + EDGE].astype(BF16)
    to_west = centre[:, cols + EDGE :].astype(BF16)
    from_west = lax.ppermute(to_east, "lon", east).astype(F32)
    from_east = lax.ppermute(to_west, "lon", west).astype(F32)
    rest = cols - EDGE
    owned = (
        centre[:, :cols]
        + jnp.pad(from_west, ((0, 0), (0, rest), (0, 0)))
        + jnp.pad(from_east, ((0, 0), (rest, 0), (0, 0)))
    )
    d_projected = jnp.concatenate([dq, owned.reshape(tokens, 2 * width).astype(BF16)], axis=1)
    grad_frame = (d_mid + nt(d_projected, weight_qkv)).astype(BF16)

    both = ("lat", "lon")
    devices = lat_n * lon_n
    swap = [(i, i ^ 1) for i in range(devices)]
    over_x, over_yz = chip_groups(lat_n, lon_n)
    n_x, n_yz = len(over_x[0]), len(over_yz[0])
    chips = n_x * n_yz

    def exchange(blocks, groups):
        return lax.all_to_all(blocks, both, 0, 0, axis_index_groups=groups)

    other, other_gain = lax.ppermute((grads[1], gains[1]), both, swap)
    held = (grads[0] + other).reshape(n_x, -1, 128)
    held_gain = (gains[0] + other_gain).reshape(n_x, -1, 128)
    n_main = held.shape[1]
    held = jnp.sum(exchange(jnp.concatenate([held, held_gain], axis=1), over_x), axis=0)
    held_gain = held[n_main:].reshape(n_yz, -1, 128)
    held = held[:n_main].reshape(n_yz, -1, 128)
    n_main = held.shape[1]
    held = jnp.sum(exchange(jnp.concatenate([held, held_gain], axis=1), over_yz), axis=0) * grad_scale
    body = held[:n_main].astype(BF16)
    gain = held[n_main:]
    high = gain.astype(BF16)
    low = (gain - high.astype(F32)).astype(BF16)
    mine = jnp.concatenate([body, high, low], axis=0)
    n_rows = mine.shape[0]
    mine = mine.reshape(1, -1, 2, 128)
    mine = exchange(jnp.broadcast_to(mine, (n_yz,) + mine.shape[1:]), over_yz)
    mine = mine.reshape((1,) + mine.shape)
    mine = exchange(jnp.broadcast_to(mine, (n_x,) + mine.shape[1:]), over_x)
    theirs = lax.ppermute(mine, both, swap)
    first = jnp.where(core == 0, mine, theirs)
    second = jnp.where(core == 0, theirs, mine)

    def unpack(field):
        flat_rows = field.reshape(chips, n_rows, 128)
        blocks = flat_rows[:, :n_main].reshape(6, 2, 256, 128)
        tail = flat_rows[:, n_main:, 0].astype(F32).reshape(chips, 2, -1)
        return blocks, (tail[:, 0] + tail[:, 1]).reshape(-1)

    first, sum_gain_attn = unpack(first)
    second, sum_gain_mlp = unpack(second)

    def beside(blocks):
        return blocks.transpose(2, 0, 1, 3).reshape(256, -1)

    return (
        block_out.reshape(rows, cols, width),
        grad_frame.reshape(rows, cols, width),
        beside(jnp.concatenate([first[5:6], second[4:6]], axis=0)),
        beside(first[4:5]),
        beside(first[:4]),
        second[:4].transpose(0, 2, 1, 3).reshape(ff, width),
        sum_gain_attn,
        sum_gain_mlp,
    )


def solution(mesh):
    return jax.shard_map(
        on_device,
        mesh=mesh,
        in_specs=(P("lat", "lon", None), P(), P(), P(), P(), P(), P(), P("lat", "lon", None)),
        out_specs=(P("lat", "lon", None), P("lat", "lon", None), P(), P(), P(), P(), P(), P()),
        check_vma=False,
    )
```

```python
import functools

import jax
import jax.numpy as jnp
from jax import lax
from jax.experimental import pallas as pl
from jax.experimental.pallas import tpu as pltpu
from jax.sharding import PartitionSpec as P

HEADS = 8
RADIUS = 6
EDGE = 8

epsilon = 1e-06
cubic_term = 0.044715
gelu_root = 0.7978845608028654
negative_big = -1e30

F32 = jnp.float32
BF16 = jnp.bfloat16


def nn(left, right):
    return lax.dot_general(left, right, (((1,), (0,)), ((), ())), preferred_element_type=F32)


def nt(left, right):
    return lax.dot_general(left, right, (((1,), (1,)), ((), ())), preferred_element_type=F32)


def gelu_pair(upward):
    tangent = jnp.tanh(gelu_root * (upward + cubic_term * upward * upward * upward))
    activated = 0.5 * upward * (1.0 + tangent)
    derivative = 0.5 * (1.0 + tangent) + 0.5 * upward * (1.0 - tangent * tangent) * gelu_root * (
        1.0 + 3.0 * cubic_term * upward * upward
    )
    return (activated, derivative)


def rms_factor(field):
    return lax.rsqrt(jnp.mean(field * field, axis=-1, keepdims=True) + epsilon)


def norm_backward(incoming, field, factor):
    mean_term = jnp.mean(incoming * field, axis=-1, keepdims=True)
    return factor * (incoming - field * factor * factor * mean_term)


def local_kernel(
    dims,
    where_ref,
    frame_ref,
    wide_ref,
    top_ref,
    bottom_ref,
    wqkv_ref,
    wproj_ref,
    gain_attn_ref,
    wup_ref,
    wdown_ref,
    gain_mlp_ref,
    cot_ref,
    block_out_ref,
    d_mid_ref,
    dq_ref,
    up_ref,
    down_ref,
    centre_ref,
    keep_ref,
    send_ref,
    grads_ref,
    halo,
    keys,
    values,
    keys_t,
    values_t,
    stack_q,
    stack_o,
    bias,
    probs,
    probs_bf,
    d_scores,
    att_t,
    dq_t,
    hidden,
    slope,
    pair_grads,
):
    rows, cols, lat_total = dims["rows"], dims["cols"], dims["lat_total"]
    heads, size, width, ff = HEADS, dims["width"] // HEADS, dims["width"], dims["ff"]
    across = cols + 2 * EDGE
    block_rows = 128 // cols
    blocks = rows // block_rows
    reach = (block_rows + 2 * RADIUS) * across
    step = block_rows * across
    pairs = heads // 2
    head_scale = size ** (-0.5)
    lat_first = where_ref[0]
    core = where_ref[1]
    side = (core, 1 - core)

    def put(index, value):
        half, row = divmod(index, 6)
        grads_ref[side[half], row * 512 : row * 512 + 256, :] = value[:, :128]
        grads_ref[side[half], row * 512 + 256 : row * 512 + 512, :] = value[:, 128:]

    def put_gain(half, terms):
        column = jnp.sum(terms.T, axis=1, keepdims=True)
        grads_ref[side[half], 3072:, :] = jnp.broadcast_to(column, (width, 128))

    rim = RADIUS * across
    inner = rows * across
    halo[0:rim, :] = top_ref[...]
    halo[rim : rim + inner, :] = wide_ref[...]
    halo[rim + inner : inner + 2 * rim, :] = bottom_ref[...]
    grid = halo[...]
    key32 = nn(grid, wqkv_ref[:, width : 2 * width])
    keys[...] = key32.astype(BF16)
    keys_t[...] = key32.T.astype(BF16)
    value32 = nn(grid, wqkv_ref[:, 2 * width :])
    values[...] = value32.astype(BF16)
    values_t[...] = value32.T.astype(BF16)

    lane_head = lax.broadcasted_iota(jnp.int32, (128, width), 1) // size

    def spread(target, field):
        for b in range(blocks):
            part = field[b * 128 : (b + 1) * 128]
            for h in range(heads):
                target[b, h * 128 : (h + 1) * 128, :] = jnp.where(lane_head == h, part, 0.0).astype(BF16)

    own = frame_ref[...]
    spread(stack_q, nn(own, wqkv_ref[:, :width]).astype(BF16).astype(F32))

    at_key = lax.broadcasted_iota(jnp.int32, (reach, 128), 0)
    at_query = lax.broadcasted_iota(jnp.int32, (reach, 128), 1)
    key_row, key_col = at_key // across, at_key % across
    key_col = jnp.where(key_col < cols + EDGE, key_col, key_col - across)
    row_gap = key_row - at_query // cols
    col_gap = key_col - at_query % cols
    near = (row_gap >= 0) & (row_gap <= 2 * RADIUS) & (col_gap >= -RADIUS) & (col_gap <= RADIUS)
    for b in range(blocks):
        row_global = key_row + (lat_first + b * block_rows - RADIUS)
        seen = near & (row_global >= 0) & (row_global < lat_total)
        bias[b] = jnp.where(seen, 0.0, negative_big)

    def diagonal(target, product, b, pair):
        at = pl.multiple_of(pair * 2 * size, 2 * size)
        lane = pl.multiple_of(b * 128, 128)
        target[pl.ds(at, size), pl.ds(lane, 128)] = product[:size, :128]
        target[pl.ds(at + size, size), pl.ds(lane, 128)] = product[size:, 128:]

    def forward(index, _):
        b, pair = index // pairs, index % pairs
        at = pl.multiple_of(pair * 256, 256)
        first = pl.multiple_of(b * step, step)
        rim_bias = bias[b]
        scores = nt(keys[pl.ds(first, reach), :], stack_q[b, pl.ds(at, 256), :]) * head_scale
        scores = scores + jnp.concatenate([rim_bias, rim_bias], axis=1)
        peak = jnp.max(scores, axis=0, keepdims=True)
        expo = jnp.exp(scores - peak)
        total = jnp.sum(expo, axis=0, keepdims=True)
        weight = expo * (1.0 / total)
        probs[index] = weight
        weight_bf = weight.astype(BF16)
        probs_bf[b, :, pl.ds(at, 256)] = weight_bf
        some = values_t[pl.ds(pl.multiple_of(pair * 2 * size, 2 * size), 2 * size), pl.ds(first, reach)]
        diagonal(att_t, nn(some, weight_bf), b, pair)
        return _

    lax.fori_loop(0, blocks * pairs, forward, 0)

    attended_t = att_t[...]
    attended = attended_t.T.astype(BF16)
    proj = nn(attended, wproj_ref[...])
    factor_one = rms_factor(proj)
    mid32 = own.astype(F32) + proj * factor_one * gain_attn_ref[...]
    mid = mid32.astype(BF16)

    downward = jnp.zeros((rows * cols, width), F32)
    for c in range(ff // 256):
        upward = nn(mid, wup_ref[:, c * 256 : (c + 1) * 256])
        activated, derivative = gelu_pair(upward)
        hidden_c = activated.astype(BF16)
        hidden[c] = activated
        slope[c] = derivative
        downward = downward + nn(hidden_c, wdown_ref[c * 256 : (c + 1) * 256, :])
    factor_two = rms_factor(downward)
    block_out_ref[...] = (mid.astype(F32) + downward * factor_two * gain_mlp_ref[...]).astype(BF16)

    incoming = cot_ref[...].astype(F32)
    put_gain(1, incoming * downward * factor_two)
    d_down = norm_backward(incoming * gain_mlp_ref[...], downward, factor_two).astype(BF16)
    mid_t = mid.astype(F32).T.astype(BF16)
    d_mid = incoming
    for c in range(ff // 256):
        d_up = (nt(d_down, wdown_ref[c * 256 : (c + 1) * 256, :]) * slope[c]).astype(BF16)
        d_mid = d_mid + nt(d_up, wup_ref[:, c * 256 : (c + 1) * 256])
        put(c, nn(mid_t, d_up))
        put(6 + c, nn(hidden[c].T.astype(BF16), d_down))
    d_mid_ref[...] = d_mid
    put_gain(0, d_mid * proj * factor_one)
    d_proj = norm_backward(d_mid * gain_attn_ref[...], proj, factor_one).astype(BF16)
    put(4, nn(attended_t.astype(BF16), d_proj))
    spread(stack_o, nt(d_proj, wproj_ref[...]).astype(BF16).astype(F32))

    def backward(index, _):
        b, pair = index // pairs, index % pairs
        at = pl.multiple_of(pair * 256, 256)
        first = pl.multiple_of(b * step, step)
        d_probs = nt(values[pl.ds(first, reach), :], stack_o[b, pl.ds(at, 256), :])
        weight = probs[index]
        d_weighted = jnp.sum(weight * d_probs, axis=0, keepdims=True)
        d_score = (weight * (d_probs - d_weighted) * head_scale).astype(BF16)
        d_scores[b, :, pl.ds(at, 256)] = d_score
        some = keys_t[pl.ds(pl.multiple_of(pair * 2 * size, 2 * size), 2 * size), pl.ds(first, reach)]
        diagonal(dq_t, nn(some, d_score), b, pair)
        return _

    lax.fori_loop(0, blocks * pairs, backward, 0)

    pair_grads[...] = jnp.zeros_like(pair_grads)
    for b in range(blocks):
        pair_grads[b * step : b * step + reach, :width] += nn(d_scores[b], stack_q[b])
        pair_grads[b * step : b * step + reach, width:] += nn(probs_bf[b], stack_o[b])

    dq = dq_t[...].T.astype(BF16)
    dq_ref[...] = dq
    up_ref[...] = pair_grads[0:rim, :].astype(BF16)
    down_ref[...] = pair_grads[rim + inner : inner + 2 * rim, :].astype(BF16)
    centre_ref[...] = pair_grads[rim : rim + inner, :]

    put(5, nn(own.astype(F32).T.astype(BF16), dq))
    grid_t = halo[...].astype(F32).T.astype(BF16)
    for half in range(2):
        terms = pair_grads[:, half * width : (half + 1) * width]
        high = terms.astype(BF16)
        low = (terms - high.astype(F32)).astype(BF16)
        put(10 + half, nn(grid_t, high) + nn(grid_t, low))
    keep_ref[...] = grads_ref[0]
    send_ref[...] = grads_ref[1]


def local_part(where, frame, wide, top, bottom, weights, cotangent, dims):
    rows, cols, width, ff = dims["rows"], dims["cols"], dims["width"], dims["ff"]
    across = cols + 2 * EDGE
    grid = (rows + 2 * RADIUS) * across
    rim = RADIUS * across
    block_rows = 128 // cols
    blocks = rows // block_rows
    reach = (block_rows + 2 * RADIUS) * across
    tokens = rows * cols
    pairs = HEADS // 2
    shape = jax.ShapeDtypeStruct
    vmem = pl.BlockSpec(memory_space=pltpu.VMEM)
    outs = [
        shape((tokens, width), BF16),
        shape((tokens, width), F32),
        shape((tokens, width), BF16),
        shape((rim, 2 * width), BF16),
        shape((rim, 2 * width), BF16),
        shape((rows * across, 2 * width), F32),
        shape((3072 + width, 128), F32),
        shape((3072 + width, 128), F32),
    ]
    return pl.pallas_call(
        functools.partial(local_kernel, dims),
        out_shape=outs,
        in_specs=[pl.BlockSpec(memory_space=pltpu.SMEM)] + [vmem] * 11,
        out_specs=[vmem] * len(outs),
        scratch_shapes=[
            pltpu.VMEM((2, 3072 + width, 128), F32),
            pltpu.VMEM((grid, width), BF16),
            pltpu.VMEM((grid, width), BF16),
            pltpu.VMEM((grid, width), BF16),
            pltpu.VMEM((width, grid), BF16),
            pltpu.VMEM((width, grid), BF16),
            pltpu.VMEM((blocks, HEADS * 128, width), BF16),
            pltpu.VMEM((blocks, HEADS * 128, width), BF16),
            pltpu.VMEM((blocks, reach, 128), F32),
            pltpu.VMEM((blocks * pairs, reach, 256), F32),
            pltpu.VMEM((blocks, reach, HEADS * 128), BF16),
            pltpu.VMEM((blocks, reach, HEADS * 128), BF16),
            pltpu.VMEM((width, tokens), F32),
            pltpu.VMEM((width, tokens), F32),
            pltpu.VMEM((ff // 256, tokens, 256), F32),
            pltpu.VMEM((ff // 256, tokens, 256), F32),
            pltpu.VMEM((grid, 2 * width), F32),
        ],
        name="local_part",
    )(where, frame, wide, top, bottom, *weights, cotangent)


def small_kernel(body, name, outs, *args):
    vmem = pl.BlockSpec(memory_space=pltpu.VMEM)
    smem = pl.BlockSpec(memory_space=pltpu.SMEM)
    return pl.pallas_call(
        body,
        out_shape=outs,
        in_specs=[smem if a.dtype == jnp.int32 else vmem for a in args],
        out_specs=jax.tree.map(lambda _: vmem, outs),
        name=name,
    )(*args)


def first_rows(shape):
    return lax.broadcasted_iota(jnp.int32, shape, 1)


def pack_chunks(n, parts_ref, chunks_ref):
    total = parts_ref[0]
    for k in range(1, parts_ref.shape[0]):
        total = total + parts_ref[k]
    deep = 512 // n
    chunks_ref[:, :deep] = total[:512].reshape(n, deep, 128)
    half = n // 2
    tail = total[512:768].reshape(half, deep, 128)
    gain = total[768:].reshape(n, -1, 128)[:, :1]
    row = first_rows(tail.shape)
    for i in range(2):
        piece = tail if i == 0 else pltpu.roll(tail, deep // 2, 1)
        mine = gain[i * half : (i + 1) * half]
        chunks_ref[i * half : (i + 1) * half, deep:] = jnp.where(row < deep // 2, piece, mine)


def finish_chunk(scale, chunks_ref, own_ref):
    n, deep = chunks_ref.shape[0], chunks_ref.shape[1] // 2
    total = jnp.sum(chunks_ref[...], axis=0) * scale
    high = total.astype(BF16).astype(F32)
    row = lax.broadcasted_iota(jnp.int32, total.shape, 0)
    total = jnp.where(row == total.shape[0] - 1, total - high, total).astype(BF16)
    own_ref[...] = jnp.broadcast_to(total[None], (n,) + total.shape)


def join_chunks(chunks_ref, rows_ref):
    n, deep = chunks_ref.shape[0], chunks_ref.shape[1] // 2
    half = n // 2
    chunks = chunks_ref[...].astype(F32)
    body = chunks[:, :deep].reshape(512, 128).astype(BF16)
    tail = chunks[:, deep:]
    row = first_rows((half, deep, 128))
    low = jnp.where(row < deep // 2, tail[:half], pltpu.roll(tail[half:], deep // 2, 1))
    low = low.reshape(256, 128).astype(BF16)
    high_gain = tail[:, deep - 2].T[:16]
    low_gain = tail[:, deep - 1].T[:16]
    gain = jnp.concatenate([high_gain, low_gain], axis=1).astype(BF16)
    for k in range(rows_ref.shape[0]):
        rows_ref[k, :512] = body
        rows_ref[k, 512:768] = low
        rows_ref[k, 768:] = gain


def unpack(where_ref, mine_ref, theirs_ref, qkv_ref, proj_ref, up_ref, down_ref, gain_attn_ref, gain_mlp_ref):
    def place(half, rows_ref, gain_ref):
        for piece in range(12):
            k, at = divmod(piece, 3)
            value = rows_ref[k, at * 256 : (at + 1) * 256, :]
            block, right = divmod(piece, 2)
            if half == 1 and block < 4:
                down_ref[block * 256 : (block + 1) * 256, right * 128 : (right + 1) * 128] = value
                continue
            target, column = up_ref, block
            if half == 1:
                target, column = qkv_ref, block - 3
            elif block == 4:
                target, column = proj_ref, 0
            elif block == 5:
                target, column = qkv_ref, 0
            lane = column * 256 + right * 128
            target[:, lane : lane + 128] = value
        for k in range(rows_ref.shape[0]):
            gain = rows_ref[k, 768:, :].astype(F32)
            gain_ref[k : k + 1, :] = (gain + pltpu.roll(gain, 64, 1))[:1]

    @pl.when(where_ref[1] == 0)
    def _():
        place(0, mine_ref, gain_attn_ref)
        place(1, theirs_ref, gain_mlp_ref)

    @pl.when(where_ref[1] == 1)
    def _():
        place(1, mine_ref, gain_mlp_ref)
        place(0, theirs_ref, gain_attn_ref)


def chip_groups(lat_n, lon_n):
    def flat(z, x, y, core):
        return (z * 2 + x // 2) * lon_n + y * 4 + x % 2 * 2 + core

    n_z, n_y = lat_n // 2, lon_n // 4
    over_x = [
        [flat(z, x, y, core) for x in range(4)] for z in range(n_z) for y in range(n_y) for core in range(2)
    ]
    over_yz = [
        [flat(z, x, y, core) for z in range(n_z) for y in range(n_y)] for x in range(4) for core in range(2)
    ]
    return over_x, over_yz


def on_device(
    frame, weight_qkv, weight_proj, gain_attn, weight_up, weight_down, gain_mlp, cotangent
):
    rows, cols, width = frame.shape
    ff = weight_up.shape[1]
    lat_n, lon_n = lax.axis_size("lat"), lax.axis_size("lon")
    tokens = rows * cols
    grad_scale = (tokens * lat_n * lon_n) ** (-0.5)
    across = cols + 2 * EDGE
    dims = {"rows": rows, "cols": cols, "width": width, "ff": ff, "lat_total": rows * lat_n}
    core = lax.axis_index("lon") % 2
    where = jnp.stack([lax.axis_index("lat") * rows, core]).astype(jnp.int32)

    east = [(i, (i + 1) % lon_n) for i in range(lon_n)]
    west = [(j, i) for i, j in east]
    south = [(i, i + 1) for i in range(lat_n - 1)]
    north = [(j, i) for i, j in south]

    from_east = lax.ppermute(frame[:, :EDGE], "lon", west)
    from_west = lax.ppermute(frame[:, cols - EDGE :], "lon", east)
    wide = jnp.concatenate([frame, from_east, from_west], axis=1)
    bottom = lax.ppermute(wide[:RADIUS], "lat", north)
    top = lax.ppermute(wide[rows - RADIUS :], "lat", south)

    weights = (
        weight_qkv,
        weight_proj,
        gain_attn.reshape(1, width),
        weight_up,
        weight_down,
        gain_mlp.reshape(1, width),
    )
    flat = (-1, width)
    block_out, d_mid, dq, up, down, centre, keep, send = local_part(
        where,
        frame.reshape(flat),
        wide.reshape(flat),
        top.reshape(flat),
        bottom.reshape(flat),
        weights,
        cotangent.reshape(flat),
        dims,
    )

    both = ("lat", "lon")
    devices = lat_n * lon_n
    swap = [(i, i ^ 1) for i in range(devices)]
    over_x, over_yz = chip_groups(lat_n, lon_n)
    n_x, n_yz = len(over_x[0]), len(over_yz[0])
    shape = jax.ShapeDtypeStruct

    def exchange(blocks, groups):
        return lax.all_to_all(blocks, both, 0, 0, axis_index_groups=groups)

    up = lax.ppermute(up, "lat", north)
    down = lax.ppermute(down, "lat", south)

    other = lax.ppermute(send, both, swap)
    pieces = (keep[:3072] + other[:3072]).reshape(n_x, 768, 128)
    tails = (keep[3072:] + other[3072:]).reshape(n_x, -1, 128)
    parts = exchange(jnp.concatenate([pieces, tails], axis=1), over_x)
    parts, up, down = lax.optimization_barrier((parts, up, down))

    up = up.reshape(RADIUS, across, 2 * width).astype(F32)
    down = down.reshape(RADIUS, across, 2 * width).astype(F32)
    rest = rows - RADIUS
    centre = centre.reshape(rows, across, 2 * width)
    centre = centre + jnp.pad(up, ((rest, 0), (0, 0), (0, 0))) + jnp.pad(down, ((0, rest), (0, 0), (0, 0)))
    to_east = centre[:, cols : cols + EDGE].astype(BF16)
    to_west = centre[:, cols + EDGE :].astype(BF16)
    from_west = lax.ppermute(to_east, "lon", east)
    from_east = lax.ppermute(to_west, "lon", west)

    deep = 2 * 512 // n_yz
    chunks = small_kernel(
        functools.partial(pack_chunks, n_yz), "pack_chunks", shape((n_yz, deep, 128), F32), parts
    )
    chunks = exchange(chunks, over_yz)
    chunks, from_west, from_east = lax.optimization_barrier((chunks, from_west, from_east))

    rest = cols - EDGE
    owned = (
        centre[:, :cols]
        + jnp.pad(from_west.astype(F32), ((0, 0), (0, rest), (0, 0)))
        + jnp.pad(from_east.astype(F32), ((0, 0), (rest, 0), (0, 0)))
    )
    d_projected = jnp.concatenate([dq, owned.reshape(tokens, 2 * width).astype(BF16)], axis=1)
    grad_frame = (d_mid + nt(d_projected, weight_qkv)).astype(BF16)

    own = small_kernel(
        functools.partial(finish_chunk, grad_scale), "finish_chunk", shape((n_yz, deep, 128), BF16), chunks
    )
    own = exchange(own, over_yz)
    mine = small_kernel(join_chunks, "join_chunks", shape((n_x, 784, 128), BF16), own)
    mine = exchange(mine, over_x)
    theirs = lax.ppermute(mine, both, swap)
    gradients = small_kernel(
        unpack,
        "unpack",
        [
            shape((width, 3 * width), BF16),
            shape((width, width), BF16),
            shape((width, ff), BF16),
            shape((ff, width), BF16),
            shape((n_x, 128), F32),
            shape((n_x, 128), F32),
        ],
        where,
        mine,
        theirs,
    )
    gain_sums = [g[:, : width // n_x].reshape(width) for g in gradients[4:]]
    return (
        block_out.reshape(rows, cols, width),
        grad_frame.reshape(rows, cols, width),
        *gradients[:4],
        *gain_sums,
    )


def solution(mesh):
    return jax.shard_map(
        on_device,
        mesh=mesh,
        in_specs=(P("lat", "lon", None), P(), P(), P(), P(), P(), P(), P("lat", "lon", None)),
        out_specs=(P("lat", "lon", None), P("lat", "lon", None), P(), P(), P(), P(), P(), P()),
        check_vma=False,
    )
```

```python
import functools

import jax
import jax.numpy as jnp
from jax import lax
from jax.experimental import pallas as pl
from jax.experimental.pallas import tpu as pltpu
from jax.sharding import PartitionSpec as P

HEADS = 8
RADIUS = 6
EDGE = 8

epsilon = 1e-06
cubic_term = 0.044715
gelu_root = 0.7978845608028654
negative_big = -1e30

F32 = jnp.float32
BF16 = jnp.bfloat16
TOP = 14.0


def nn(left, right):
    return lax.dot_general(left, right, (((1,), (0,)), ((), ())), preferred_element_type=F32)


def nt(left, right):
    return lax.dot_general(left, right, (((1,), (1,)), ((), ())), preferred_element_type=F32)


def gelu_pair(upward):
    tangent = jnp.tanh(gelu_root * (upward + cubic_term * upward * upward * upward))
    activated = 0.5 * upward * (1.0 + tangent)
    derivative = 0.5 * (1.0 + tangent) + 0.5 * upward * (1.0 - tangent * tangent) * gelu_root * (
        1.0 + 3.0 * cubic_term * upward * upward
    )
    return (activated, derivative)


def rms_factor(field):
    return lax.rsqrt(jnp.mean(field * field, axis=-1, keepdims=True) + epsilon)


def norm_backward(incoming, field, factor):
    mean_term = jnp.mean(incoming * field, axis=-1, keepdims=True)
    return factor * (incoming - field * factor * factor * mean_term)


def local_kernel(
    dims,
    where_ref,
    frame_ref,
    wide_ref,
    top_ref,
    bottom_ref,
    wqkv_ref,
    wproj_ref,
    gain_attn_ref,
    wup_ref,
    wdown_ref,
    gain_mlp_ref,
    cot_ref,
    block_out_ref,
    d_mid_ref,
    dq_ref,
    up_ref,
    down_ref,
    centre_ref,
    keep_ref,
    send_ref,
    grads_ref,
    halo,
    keys,
    values,
    keys_t,
    values_t,
    stack_q,
    stack_o,
    bias,
    probs,
    probs_bf,
    d_scores,
    att_t,
    dq_t,
    hidden,
    slope,
    pair_grads,
):
    rows, cols, lat_total = dims["rows"], dims["cols"], dims["lat_total"]
    heads, size, width, ff = HEADS, dims["width"] // HEADS, dims["width"], dims["ff"]
    across = cols + 2 * EDGE
    block_rows = 128 // cols
    blocks = rows // block_rows
    reach = (block_rows + 2 * RADIUS) * across
    step = block_rows * across
    pairs = heads // 2
    head_scale = size ** (-0.5)
    lat_first = where_ref[0]
    core = where_ref[1]
    side = (core, 1 - core)

    def put(index, value):
        half, row = divmod(index, 6)
        grads_ref[side[half], row * 512 : row * 512 + 256, :] = value[:, :128]
        grads_ref[side[half], row * 512 + 256 : row * 512 + 512, :] = value[:, 128:]

    def put_gain(half, terms):
        column = jnp.sum(terms.T, axis=1, keepdims=True)
        grads_ref[side[half], 3072:, :] = jnp.broadcast_to(column, (width, 128))

    rim = RADIUS * across
    inner = rows * across
    halo[0:rim, :] = top_ref[...]
    halo[rim : rim + inner, :] = wide_ref[...]
    halo[rim + inner : inner + 2 * rim, :] = bottom_ref[...]
    grid = halo[...]
    key32 = nn(grid, wqkv_ref[:, width : 2 * width])
    keys[...] = key32.astype(BF16)
    keys_t[...] = key32.T.astype(BF16)
    value32 = nn(grid, wqkv_ref[:, 2 * width :])
    values[...] = value32.astype(BF16)
    values_t[...] = value32.T.astype(BF16)

    lane_head = lax.broadcasted_iota(jnp.int32, (128, width), 1) // size

    def spread(target, field):
        for b in range(blocks):
            part = field[b * 128 : (b + 1) * 128]
            for h in range(heads):
                target[b, h * 128 : (h + 1) * 128, :] = jnp.where(lane_head == h, part, 0.0).astype(BF16)

    own = frame_ref[...]
    spread(stack_q, nn(own, wqkv_ref[:, :width]).astype(BF16).astype(F32))

    at_key = lax.broadcasted_iota(jnp.int32, (reach, 128), 0)
    at_query = lax.broadcasted_iota(jnp.int32, (reach, 128), 1)
    key_row, key_col = at_key // across, at_key % across
    key_col = jnp.where(key_col < cols + EDGE, key_col, key_col - across)
    row_gap = key_row - at_query // cols
    col_gap = key_col - at_query % cols
    near = (row_gap >= 0) & (row_gap <= 2 * RADIUS) & (col_gap >= -RADIUS) & (col_gap <= RADIUS)
    for b in range(blocks):
        row_global = key_row + (lat_first + b * block_rows - RADIUS)
        seen = near & (row_global >= 0) & (row_global < lat_total)
        bias[b] = jnp.where(seen, 0.0, negative_big)

    def diagonal(target, product, b, pair):
        at = pl.multiple_of(pair * 2 * size, 2 * size)
        lane = pl.multiple_of(b * 128, 128)
        target[pl.ds(at, size), pl.ds(lane, 128)] = product[:size, :128]
        target[pl.ds(at + size, size), pl.ds(lane, 128)] = product[size:, 128:]

    def forward(index, _):
        b, pair = index // pairs, index % pairs
        at = pl.multiple_of(pair * 256, 256)
        first = pl.multiple_of(b * step, step)
        rim_bias = bias[b]
        scores = nt(keys[pl.ds(first, reach), :], stack_q[b, pl.ds(at, 256), :]) * head_scale
        scores = scores + jnp.concatenate([rim_bias, rim_bias], axis=1)
        peak = jnp.max(scores, axis=0, keepdims=True)
        expo = jnp.exp(scores - peak)
        total = jnp.sum(expo, axis=0, keepdims=True)
        weight = expo * (1.0 / total)
        probs[index] = weight
        weight_bf = weight.astype(BF16)
        probs_bf[b, :, pl.ds(at, 256)] = weight_bf
        some = values_t[pl.ds(pl.multiple_of(pair * 2 * size, 2 * size), 2 * size), pl.ds(first, reach)]
        diagonal(att_t, nn(some, weight_bf), b, pair)
        return _

    lax.fori_loop(0, blocks * pairs, forward, 0)

    attended_t = att_t[...]
    attended = attended_t.T.astype(BF16)
    proj = nn(attended, wproj_ref[...])
    factor_one = rms_factor(proj)
    mid32 = own.astype(F32) + proj * factor_one * gain_attn_ref[...]
    mid = mid32.astype(BF16)

    downward = jnp.zeros((rows * cols, width), F32)
    for c in range(ff // 256):
        upward = nn(mid, wup_ref[:, c * 256 : (c + 1) * 256])
        activated, derivative = gelu_pair(upward)
        hidden_c = activated.astype(BF16)
        hidden[c] = activated
        slope[c] = derivative
        downward = downward + nn(hidden_c, wdown_ref[c * 256 : (c + 1) * 256, :])
    factor_two = rms_factor(downward)
    block_out_ref[...] = (mid.astype(F32) + downward * factor_two * gain_mlp_ref[...]).astype(BF16)

    incoming = cot_ref[...].astype(F32)
    put_gain(1, incoming * downward * factor_two)
    d_down = norm_backward(incoming * gain_mlp_ref[...], downward, factor_two).astype(BF16)
    mid_t = mid.astype(F32).T.astype(BF16)
    d_mid = incoming
    for c in range(ff // 256):
        d_up = (nt(d_down, wdown_ref[c * 256 : (c + 1) * 256, :]) * slope[c]).astype(BF16)
        d_mid = d_mid + nt(d_up, wup_ref[:, c * 256 : (c + 1) * 256])
        put(c, nn(mid_t, d_up))
        put(6 + c, nn(hidden[c].T.astype(BF16), d_down))
    d_mid_ref[...] = d_mid
    put_gain(0, d_mid * proj * factor_one)
    d_proj = norm_backward(d_mid * gain_attn_ref[...], proj, factor_one).astype(BF16)
    put(4, nn(attended_t.astype(BF16), d_proj))
    spread(stack_o, nt(d_proj, wproj_ref[...]).astype(BF16).astype(F32))

    def backward(index, _):
        b, pair = index // pairs, index % pairs
        at = pl.multiple_of(pair * 256, 256)
        first = pl.multiple_of(b * step, step)
        d_probs = nt(values[pl.ds(first, reach), :], stack_o[b, pl.ds(at, 256), :])
        weight = probs[index]
        d_weighted = jnp.sum(weight * d_probs, axis=0, keepdims=True)
        d_score = (weight * (d_probs - d_weighted) * head_scale).astype(BF16)
        d_scores[b, :, pl.ds(at, 256)] = d_score
        some = keys_t[pl.ds(pl.multiple_of(pair * 2 * size, 2 * size), 2 * size), pl.ds(first, reach)]
        diagonal(dq_t, nn(some, d_score), b, pair)
        return _

    lax.fori_loop(0, blocks * pairs, backward, 0)

    pair_grads[...] = jnp.zeros_like(pair_grads)
    for b in range(blocks):
        pair_grads[b * step : b * step + reach, :width] += nn(d_scores[b], stack_q[b])
        pair_grads[b * step : b * step + reach, width:] += nn(probs_bf[b], stack_o[b])

    dq = dq_t[...].T.astype(BF16)
    dq_ref[...] = dq
    up_ref[...] = pair_grads[0:rim, :].astype(BF16)
    down_ref[...] = pair_grads[rim + inner : inner + 2 * rim, :].astype(BF16)
    centre_ref[...] = pair_grads[rim : rim + inner, :]

    put(5, nn(own.astype(F32).T.astype(BF16), dq))
    grid_t = halo[...].astype(F32).T.astype(BF16)
    for half in range(2):
        terms = pair_grads[:, half * width : (half + 1) * width]
        high = terms.astype(BF16)
        low = (terms - high.astype(F32)).astype(BF16)
        put(10 + half, nn(grid_t, high) + nn(grid_t, low))
    keep_ref[...] = grads_ref[0]
    send_ref[...] = grads_ref[1]


def local_part(where, frame, wide, top, bottom, weights, cotangent, dims):
    rows, cols, width, ff = dims["rows"], dims["cols"], dims["width"], dims["ff"]
    across = cols + 2 * EDGE
    grid = (rows + 2 * RADIUS) * across
    rim = RADIUS * across
    block_rows = 128 // cols
    blocks = rows // block_rows
    reach = (block_rows + 2 * RADIUS) * across
    tokens = rows * cols
    pairs = HEADS // 2
    shape = jax.ShapeDtypeStruct
    vmem = pl.BlockSpec(memory_space=pltpu.VMEM)
    outs = [
        shape((tokens, width), BF16),
        shape((tokens, width), F32),
        shape((tokens, width), BF16),
        shape((rim, 2 * width), BF16),
        shape((rim, 2 * width), BF16),
        shape((rows * across, 2 * width), F32),
        shape((3072 + width, 128), F32),
        shape((3072 + width, 128), F32),
    ]
    return pl.pallas_call(
        functools.partial(local_kernel, dims),
        out_shape=outs,
        in_specs=[pl.BlockSpec(memory_space=pltpu.SMEM)] + [vmem] * 11,
        out_specs=[vmem] * len(outs),
        scratch_shapes=[
            pltpu.VMEM((2, 3072 + width, 128), F32),
            pltpu.VMEM((grid, width), BF16),
            pltpu.VMEM((grid, width), BF16),
            pltpu.VMEM((grid, width), BF16),
            pltpu.VMEM((width, grid), BF16),
            pltpu.VMEM((width, grid), BF16),
            pltpu.VMEM((blocks, HEADS * 128, width), BF16),
            pltpu.VMEM((blocks, HEADS * 128, width), BF16),
            pltpu.VMEM((blocks, reach, 128), F32),
            pltpu.VMEM((blocks * pairs, reach, 256), F32),
            pltpu.VMEM((blocks, reach, HEADS * 128), BF16),
            pltpu.VMEM((blocks, reach, HEADS * 128), BF16),
            pltpu.VMEM((width, tokens), F32),
            pltpu.VMEM((width, tokens), F32),
            pltpu.VMEM((ff // 256, tokens, 256), F32),
            pltpu.VMEM((ff // 256, tokens, 256), F32),
            pltpu.VMEM((grid, 2 * width), F32),
        ],
        name="local_part",
    )(where, frame, wide, top, bottom, *weights, cotangent)


def small_kernel(body, name, outs, *args):
    vmem = pl.BlockSpec(memory_space=pltpu.VMEM)
    smem = pl.BlockSpec(memory_space=pltpu.SMEM)
    return pl.pallas_call(
        body,
        out_shape=outs,
        in_specs=[smem if a.dtype == jnp.int32 else vmem for a in args],
        out_specs=jax.tree.map(lambda _: vmem, outs),
        name=name,
    )(*args)


def first_rows(shape):
    return lax.broadcasted_iota(jnp.int32, shape, 1)


def pack_chunks(keep_ref, other_ref, chunks_ref):
    n = chunks_ref.shape[0] // 4
    half = n // 2

    def scaled(value):
        largest = jnp.maximum(jnp.max(jnp.abs(value), axis=(0, 1), keepdims=True), 1e-37)
        power = jnp.clip(jnp.ceil(jnp.log2(largest)), -100.0, 127.0)
        return value * jnp.exp2(TOP - power), power

    gain, gain_power = scaled(keep_ref[3072:, :] + other_ref[3072:, :])
    gain = gain.reshape(4, n, 1, 128)
    row = lax.broadcasted_iota(jnp.int32, (half, 8, 128), 1)
    for k in range(4):
        first = k * 768
        powers = []
        for i in range(2):
            at = first + i * 256
            value, power = scaled(keep_ref[at : at + 256, :] + other_ref[at : at + 256, :])
            powers.append(power)
            chunks_ref[k * n + i * half : k * n + (i + 1) * half, :8] = value.reshape(half, 8, 128)
        at = first + 512
        tail, tail_power = scaled(keep_ref[at : at + 256, :] + other_ref[at : at + 256, :])
        tail = tail.reshape(half, 8, 128)
        for i in range(2):
            piece = tail if i == 0 else pltpu.roll(tail, 4, 1)
            piece = jnp.where(row < 4, piece, gain[k, i * half : (i + 1) * half])
            for at_row, power in ((5, powers[i]), (6, tail_power), (7, gain_power)):
                piece = jnp.where(row == at_row, power.reshape(1, 1, 1), piece)
            chunks_ref[k * n + i * half : k * n + (i + 1) * half, 8:] = piece


def finish_chunk(scale, chunks_ref, own_ref):
    body = chunks_ref[:, :8]
    tail = chunks_ref[:, 8:]
    factor = jnp.exp2(tail - TOP)
    body = jnp.sum(body * factor[:, 5:6], axis=0)
    row = lax.broadcasted_iota(jnp.int32, tail.shape, 1)
    factor = jnp.where(row < 4, factor[:, 6:7], factor[:, 7:8])
    tail = jnp.sum(jnp.where(row < 5, tail * factor, 0.0), axis=0) * scale
    gain = tail[4:5]
    high = gain.astype(BF16).astype(F32)
    row = lax.broadcasted_iota(jnp.int32, tail.shape, 0)
    tail = jnp.where(row == 6, high, jnp.where(row == 7, gain - high, tail))
    total = jnp.concatenate([body * scale, tail], axis=0).astype(BF16)
    own_ref[...] = jnp.broadcast_to(total[None], own_ref.shape)


def join_chunks(chunks_ref, rows_ref):
    n, deep = chunks_ref.shape[0], chunks_ref.shape[1] // 2
    half = n // 2
    chunks = chunks_ref[...].astype(F32)
    body = chunks[:, :deep].reshape(512, 128).astype(BF16)
    tail = chunks[:, deep:]
    row = first_rows((half, deep, 128))
    low = jnp.where(row < deep // 2, tail[:half], pltpu.roll(tail[half:], deep // 2, 1))
    low = low.reshape(256, 128).astype(BF16)
    high_gain = tail[:, deep - 2].T[:16]
    low_gain = tail[:, deep - 1].T[:16]
    gain = jnp.concatenate([high_gain, low_gain], axis=1).astype(BF16)
    for k in range(rows_ref.shape[0]):
        rows_ref[k, :512] = body
        rows_ref[k, 512:768] = low
        rows_ref[k, 768:] = gain


def unpack(where_ref, mine_ref, theirs_ref, qkv_ref, proj_ref, up_ref, down_ref, gain_attn_ref, gain_mlp_ref):
    def place(half, rows_ref, gain_ref):
        for piece in range(12):
            k, at = divmod(piece, 3)
            value = rows_ref[k, at * 256 : (at + 1) * 256, :]
            block, right = divmod(piece, 2)
            if half == 1 and block < 4:
                down_ref[block * 256 : (block + 1) * 256, right * 128 : (right + 1) * 128] = value
                continue
            target, column = up_ref, block
            if half == 1:
                target, column = qkv_ref, block - 3
            elif block == 4:
                target, column = proj_ref, 0
            elif block == 5:
                target, column = qkv_ref, 0
            lane = column * 256 + right * 128
            target[:, lane : lane + 128] = value
        lane = lax.broadcasted_iota(jnp.int32, (16, 128), 1)
        for k in range(0, rows_ref.shape[0], 2):
            gain = [rows_ref[k + i, 768:, :].astype(F32) for i in range(2)]
            gain = [g + pltpu.roll(g, 64, 1) for g in gain]
            gain_ref[:, k * 64 : k * 64 + 128] = jnp.where(lane < 64, *gain)[:1]

    @pl.when(where_ref[1] == 0)
    def _():
        place(0, mine_ref, gain_attn_ref)
        place(1, theirs_ref, gain_mlp_ref)

    @pl.when(where_ref[1] == 1)
    def _():
        place(1, mine_ref, gain_mlp_ref)
        place(0, theirs_ref, gain_attn_ref)


def chip_groups(lat_n, lon_n):
    def flat(z, x, y, core):
        return (z * 2 + x // 2) * lon_n + y * 4 + x % 2 * 2 + core

    n_z, n_y = lat_n // 2, lon_n // 4
    over_x = [
        [flat(z, x, y, core) for x in range(4)] for z in range(n_z) for y in range(n_y) for core in range(2)
    ]
    over_yz = [
        [flat(z, x, y, core) for z in range(n_z) for y in range(n_y)] for x in range(4) for core in range(2)
    ]
    over_chips = [
        [flat(z, x, y, core) for x in range(4) for z in range(n_z) for y in range(n_y)] for core in range(2)
    ]
    return over_x, over_yz, over_chips


def on_device(
    frame, weight_qkv, weight_proj, gain_attn, weight_up, weight_down, gain_mlp, cotangent
):
    rows, cols, width = frame.shape
    ff = weight_up.shape[1]
    lat_n, lon_n = lax.axis_size("lat"), lax.axis_size("lon")
    tokens = rows * cols
    grad_scale = (tokens * lat_n * lon_n) ** (-0.5)
    across = cols + 2 * EDGE
    dims = {"rows": rows, "cols": cols, "width": width, "ff": ff, "lat_total": rows * lat_n}
    core = lax.axis_index("lon") % 2
    where = jnp.stack([lax.axis_index("lat") * rows, core]).astype(jnp.int32)

    east = [(i, (i + 1) % lon_n) for i in range(lon_n)]
    west = [(j, i) for i, j in east]
    south = [(i, i + 1) for i in range(lat_n - 1)]
    north = [(j, i) for i, j in south]

    from_east = lax.ppermute(frame[:, :EDGE], "lon", west)
    from_west = lax.ppermute(frame[:, cols - EDGE :], "lon", east)
    wide = jnp.concatenate([frame, from_east, from_west], axis=1)
    bottom = lax.ppermute(wide[:RADIUS], "lat", north)
    top = lax.ppermute(wide[rows - RADIUS :], "lat", south)

    weights = (
        weight_qkv,
        weight_proj,
        gain_attn.reshape(1, width),
        weight_up,
        weight_down,
        gain_mlp.reshape(1, width),
    )
    flat = (-1, width)
    block_out, d_mid, dq, up, down, centre, keep, send = local_part(
        where,
        frame.reshape(flat),
        wide.reshape(flat),
        top.reshape(flat),
        bottom.reshape(flat),
        weights,
        cotangent.reshape(flat),
        dims,
    )

    both = ("lat", "lon")
    devices = lat_n * lon_n
    swap = [(i, i ^ 1) for i in range(devices)]
    over_x, over_yz, over_chips = chip_groups(lat_n, lon_n)
    n_x, n_yz = len(over_x[0]), len(over_yz[0])
    shape = jax.ShapeDtypeStruct

    def exchange(blocks, groups):
        return lax.all_to_all(blocks, both, 0, 0, axis_index_groups=groups)

    up = lax.ppermute(up, "lat", north)
    down = lax.ppermute(down, "lat", south)

    other = lax.ppermute(send, both, swap)
    chunks = small_kernel(pack_chunks, "pack_chunks", shape((n_x * n_yz, 16, 128), F32), keep, other)
    chunks = exchange(chunks.astype(jnp.float16), over_chips)
    chunks, up, down = lax.optimization_barrier((chunks, up, down))

    up = up.reshape(RADIUS, across, 2 * width).astype(F32)
    down = down.reshape(RADIUS, across, 2 * width).astype(F32)
    rest = rows - RADIUS
    centre = centre.reshape(rows, across, 2 * width)
    centre = centre + jnp.pad(up, ((rest, 0), (0, 0), (0, 0))) + jnp.pad(down, ((0, rest), (0, 0), (0, 0)))
    to_east = centre[:, cols : cols + EDGE].astype(BF16)
    to_west = centre[:, cols + EDGE :].astype(BF16)
    from_west = lax.ppermute(to_east, "lon", east)
    from_east = lax.ppermute(to_west, "lon", west)

    own = small_kernel(
        functools.partial(finish_chunk, grad_scale),
        "finish_chunk",
        shape((n_yz, 16, 128), BF16),
        chunks.astype(F32),
    )
    own = exchange(own, over_yz)
    own, from_west, from_east = lax.optimization_barrier((own, from_west, from_east))

    rest = cols - EDGE
    owned = (
        centre[:, :cols]
        + jnp.pad(from_west.astype(F32), ((0, 0), (0, rest), (0, 0)))
        + jnp.pad(from_east.astype(F32), ((0, 0), (rest, 0), (0, 0)))
    )
    d_projected = jnp.concatenate([dq, owned.reshape(tokens, 2 * width).astype(BF16)], axis=1)
    grad_frame = (d_mid + nt(d_projected, weight_qkv)).astype(BF16)

    mine = small_kernel(join_chunks, "join_chunks", shape((n_x, 784, 128), BF16), own)
    mine = exchange(mine, over_x)
    theirs = lax.ppermute(mine, both, swap)
    gradients = small_kernel(
        unpack,
        "unpack",
        [
            shape((width, 3 * width), BF16),
            shape((width, width), BF16),
            shape((width, ff), BF16),
            shape((ff, width), BF16),
            shape((1, width), F32),
            shape((1, width), F32),
        ],
        where,
        mine,
        theirs,
    )
    gain_sums = [g.reshape(width) for g in gradients[4:]]
    return (
        block_out.reshape(rows, cols, width),
        grad_frame.reshape(rows, cols, width),
        *gradients[:4],
        *gain_sums,
    )


def solution(mesh):
    return jax.shard_map(
        on_device,
        mesh=mesh,
        in_specs=(P("lat", "lon", None), P(), P(), P(), P(), P(), P(), P("lat", "lon", None)),
        out_specs=(P("lat", "lon", None), P("lat", "lon", None), P(), P(), P(), P(), P(), P()),
        check_vma=False,
    )
```

```python
import functools

import jax
import jax.numpy as jnp
from jax import lax
from jax.experimental import pallas as pl
from jax.experimental.pallas import tpu as pltpu
from jax.sharding import PartitionSpec as P


HEADS = 8
RADIUS = 6
EDGE = 8

epsilon = 1e-06
cubic_term = 0.044715
gelu_root = 0.7978845608028654
negative_big = -1e30

F32 = jnp.float32
BF16 = jnp.bfloat16


def nn(left, right):
    return lax.dot_general(left, right, (((1,), (0,)), ((), ())), preferred_element_type=F32)


def nt(left, right):
    return lax.dot_general(left, right, (((1,), (1,)), ((), ())), preferred_element_type=F32)


def gelu_pair(upward):
    tangent = jnp.tanh(gelu_root * (upward + cubic_term * upward * upward * upward))
    activated = 0.5 * upward * (1.0 + tangent)
    derivative = 0.5 * (1.0 + tangent) + 0.5 * upward * (1.0 - tangent * tangent) * gelu_root * (
        1.0 + 3.0 * cubic_term * upward * upward
    )
    return (activated, derivative)


def rms_factor(field):
    return lax.rsqrt(jnp.mean(field * field, axis=-1, keepdims=True) + epsilon)


def norm_backward(incoming, field, factor):
    mean_term = jnp.mean(incoming * field, axis=-1, keepdims=True)
    return factor * (incoming - field * factor * factor * mean_term)


def local_kernel(
    dims,
    where_ref,
    frame_ref,
    wide_ref,
    top_ref,
    bottom_ref,
    wqkv_ref,
    wproj_ref,
    gain_attn_ref,
    wup_ref,
    wdown_ref,
    gain_mlp_ref,
    cot_ref,
    block_out_ref,
    d_mid_ref,
    dq_ref,
    up_ref,
    down_ref,
    centre_ref,
    keep_ref,
    send_ref,
    grads_ref,
    halo,
    keys,
    values,
    keys_t,
    values_t,
    stack_q,
    stack_o,
    bias,
    probs,
    probs_bf,
    d_scores,
    att_t,
    dq_t,
    hidden,
    slope,
    pair_grads,
):
    rows, cols, lat_total = dims["rows"], dims["cols"], dims["lat_total"]
    heads, size, width, ff = HEADS, dims["width"] // HEADS, dims["width"], dims["ff"]
    across = cols + 2 * EDGE
    block_rows = 128 // cols
    blocks = rows // block_rows
    reach = (block_rows + 2 * RADIUS) * across
    step = block_rows * across
    pairs = heads // 2
    head_scale = size ** (-0.5)
    lat_first = where_ref[0]
    core = where_ref[1]
    side = (core, 1 - core)

    def put(index, value):
        half, block = divmod(index, 6)
        for right in range(2):
            k, at = divmod(2 * block + right, 3)
            grads_ref[side[half], k, at * 256 : (at + 1) * 256, :] = value[:, right * 128 : (right + 1) * 128]

    def put_gain(half, terms):
        column = jnp.broadcast_to(jnp.sum(terms.T, axis=1, keepdims=True), (width, 128))
        each = width // 4
        for k in range(4):
            grads_ref[side[half], k, 768:, :] = column[k * each : (k + 1) * each]

    rim = RADIUS * across
    inner = rows * across
    halo[0:rim, :] = top_ref[...]
    halo[rim : rim + inner, :] = wide_ref[...]
    halo[rim + inner : inner + 2 * rim, :] = bottom_ref[...]
    grid = halo[...]
    key32 = nn(grid, wqkv_ref[:, width : 2 * width])
    keys[...] = key32.astype(BF16)
    keys_t[...] = key32.T.astype(BF16)
    value32 = nn(grid, wqkv_ref[:, 2 * width :])
    values[...] = value32.astype(BF16)
    values_t[...] = value32.T.astype(BF16)

    lane_head = lax.broadcasted_iota(jnp.int32, (128, width), 1) // size

    def spread(target, field):
        for b in range(blocks):
            part = field[b * 128 : (b + 1) * 128]
            for h in range(heads):
                target[b, h * 128 : (h + 1) * 128, :] = jnp.where(lane_head == h, part, 0.0).astype(BF16)

    own = frame_ref[...]
    spread(stack_q, nn(own, wqkv_ref[:, :width]).astype(BF16).astype(F32))

    at_key = lax.broadcasted_iota(jnp.int32, (reach, 128), 0)
    at_query = lax.broadcasted_iota(jnp.int32, (reach, 128), 1)
    key_row, key_col = at_key // across, at_key % across
    key_col = jnp.where(key_col < cols + EDGE, key_col, key_col - across)
    row_gap = key_row - at_query // cols
    col_gap = key_col - at_query % cols
    near = (row_gap >= 0) & (row_gap <= 2 * RADIUS) & (col_gap >= -RADIUS) & (col_gap <= RADIUS)
    for b in range(blocks):
        row_global = key_row + (lat_first + b * block_rows - RADIUS)
        seen = near & (row_global >= 0) & (row_global < lat_total)
        bias[b] = jnp.where(seen, 0.0, negative_big)

    def diagonal(target, product, b, pair):
        at = pl.multiple_of(pair * 2 * size, 2 * size)
        lane = pl.multiple_of(b * 128, 128)
        target[pl.ds(at, size), pl.ds(lane, 128)] = product[:size, :128]
        target[pl.ds(at + size, size), pl.ds(lane, 128)] = product[size:, 128:]

    def forward(index, _):
        b, pair = index // pairs, index % pairs
        at = pl.multiple_of(pair * 256, 256)
        first = pl.multiple_of(b * step, step)
        rim_bias = bias[b]
        scores = nt(keys[pl.ds(first, reach), :], stack_q[b, pl.ds(at, 256), :]) * head_scale
        scores = scores + jnp.concatenate([rim_bias, rim_bias], axis=1)
        peak = jnp.max(scores, axis=0, keepdims=True)
        expo = jnp.exp(scores - peak)
        total = jnp.sum(expo, axis=0, keepdims=True)
        weight = expo * (1.0 / total)
        probs[index] = weight
        weight_bf = weight.astype(BF16)
        probs_bf[b, :, pl.ds(at, 256)] = weight_bf
        some = values_t[pl.ds(pl.multiple_of(pair * 2 * size, 2 * size), 2 * size), pl.ds(first, reach)]
        diagonal(att_t, nn(some, weight_bf), b, pair)
        return _

    lax.fori_loop(0, blocks * pairs, forward, 0)

    attended_t = att_t[...]
    attended = attended_t.T.astype(BF16)
    proj = nn(attended, wproj_ref[...])
    factor_one = rms_factor(proj)
    mid32 = own.astype(F32) + proj * factor_one * gain_attn_ref[...]
    mid = mid32.astype(BF16)

    downward = jnp.zeros((rows * cols, width), F32)
    for c in range(ff // 256):
        upward = nn(mid, wup_ref[:, c * 256 : (c + 1) * 256])
        activated, derivative = gelu_pair(upward)
        hidden_c = activated.astype(BF16)
        hidden[c] = activated
        slope[c] = derivative
        downward = downward + nn(hidden_c, wdown_ref[c * 256 : (c + 1) * 256, :])
    factor_two = rms_factor(downward)
    block_out_ref[...] = (mid.astype(F32) + downward * factor_two * gain_mlp_ref[...]).astype(BF16)

    incoming = cot_ref[...].astype(F32)
    put_gain(1, incoming * downward * factor_two)
    d_down = norm_backward(incoming * gain_mlp_ref[...], downward, factor_two).astype(BF16)
    mid_t = mid.astype(F32).T.astype(BF16)
    d_mid = incoming
    for c in range(ff // 256):
        d_up = (nt(d_down, wdown_ref[c * 256 : (c + 1) * 256, :]) * slope[c]).astype(BF16)
        d_mid = d_mid + nt(d_up, wup_ref[:, c * 256 : (c + 1) * 256])
        put(c, nn(mid_t, d_up))
        put(6 + c, nn(hidden[c].T.astype(BF16), d_down))
    d_mid_ref[...] = d_mid
    put_gain(0, d_mid * proj * factor_one)
    d_proj = norm_backward(d_mid * gain_attn_ref[...], proj, factor_one).astype(BF16)
    put(4, nn(attended_t.astype(BF16), d_proj))
    spread(stack_o, nt(d_proj, wproj_ref[...]).astype(BF16).astype(F32))

    def backward(index, _):
        b, pair = index // pairs, index % pairs
        at = pl.multiple_of(pair * 256, 256)
        first = pl.multiple_of(b * step, step)
        d_probs = nt(values[pl.ds(first, reach), :], stack_o[b, pl.ds(at, 256), :])
        weight = probs[index]
        d_weighted = jnp.sum(weight * d_probs, axis=0, keepdims=True)
        d_score = (weight * (d_probs - d_weighted) * head_scale).astype(BF16)
        d_scores[b, :, pl.ds(at, 256)] = d_score
        some = keys_t[pl.ds(pl.multiple_of(pair * 2 * size, 2 * size), 2 * size), pl.ds(first, reach)]
        diagonal(dq_t, nn(some, d_score), b, pair)
        return _

    lax.fori_loop(0, blocks * pairs, backward, 0)

    pair_grads[...] = jnp.zeros_like(pair_grads)
    for b in range(blocks):
        pair_grads[b * step : b * step + reach, :width] += nn(d_scores[b], stack_q[b])
        pair_grads[b * step : b * step + reach, width:] += nn(probs_bf[b], stack_o[b])

    dq = dq_t[...].T.astype(BF16)
    dq_ref[...] = dq
    up_ref[...] = pair_grads[0:rim, :].astype(BF16)
    down_ref[...] = pair_grads[rim + inner : inner + 2 * rim, :].astype(BF16)
    centre_ref[...] = pair_grads[rim : rim + inner, :]

    put(5, nn(own.astype(F32).T.astype(BF16), dq))
    grid_t = halo[...].astype(F32).T.astype(BF16)
    for half in range(2):
        terms = pair_grads[:, half * width : (half + 1) * width]
        high = terms.astype(BF16)
        low = (terms - high.astype(F32)).astype(BF16)
        put(10 + half, nn(grid_t, high) + nn(grid_t, low))
    keep_ref[...] = grads_ref[0]
    send_ref[...] = grads_ref[1]


def local_part(where, frame, wide, top, bottom, weights, cotangent, dims):
    rows, cols, width, ff = dims["rows"], dims["cols"], dims["width"], dims["ff"]
    across = cols + 2 * EDGE
    grid = (rows + 2 * RADIUS) * across
    rim = RADIUS * across
    block_rows = 128 // cols
    blocks = rows // block_rows
    reach = (block_rows + 2 * RADIUS) * across
    tokens = rows * cols
    pairs = HEADS // 2
    shape = jax.ShapeDtypeStruct
    vmem = pl.BlockSpec(memory_space=pltpu.VMEM)
    outs = [
        shape((tokens, width), BF16),
        shape((tokens, width), F32),
        shape((tokens, width), BF16),
        shape((rim, 2 * width), BF16),
        shape((rim, 2 * width), BF16),
        shape((rows * across, 2 * width), F32),
        shape((4, 768 + width // 4, 128), F32),
        shape((4, 768 + width // 4, 128), F32),
    ]
    return pl.pallas_call(
        functools.partial(local_kernel, dims),
        out_shape=outs,
        in_specs=[pl.BlockSpec(memory_space=pltpu.SMEM)] + [vmem] * 11,
        out_specs=[vmem] * len(outs),
        scratch_shapes=[
            pltpu.VMEM((2, 4, 768 + width // 4, 128), F32),
            pltpu.VMEM((grid, width), BF16),
            pltpu.VMEM((grid, width), BF16),
            pltpu.VMEM((grid, width), BF16),
            pltpu.VMEM((width, grid), BF16),
            pltpu.VMEM((width, grid), BF16),
            pltpu.VMEM((blocks, HEADS * 128, width), BF16),
            pltpu.VMEM((blocks, HEADS * 128, width), BF16),
            pltpu.VMEM((blocks, reach, 128), F32),
            pltpu.VMEM((blocks * pairs, reach, 256), F32),
            pltpu.VMEM((blocks, reach, HEADS * 128), BF16),
            pltpu.VMEM((blocks, reach, HEADS * 128), BF16),
            pltpu.VMEM((width, tokens), F32),
            pltpu.VMEM((width, tokens), F32),
            pltpu.VMEM((ff // 256, tokens, 256), F32),
            pltpu.VMEM((ff // 256, tokens, 256), F32),
            pltpu.VMEM((grid, 2 * width), F32),
        ],
        name="local_part",
    )(where, frame, wide, top, bottom, *weights, cotangent)


def small_kernel(body, outs, *args, scratch=()):
    vmem = pl.BlockSpec(memory_space=pltpu.VMEM)
    smem = pl.BlockSpec(memory_space=pltpu.SMEM)
    return pl.pallas_call(
        body,
        out_shape=outs,
        in_specs=[smem if a.dtype == jnp.int32 else vmem for a in args],
        out_specs=jax.tree.map(lambda _: vmem, outs),
        scratch_shapes=scratch,
    )(*args)


def first_rows(shape):
    return lax.broadcasted_iota(jnp.int32, shape, 1)


def deal_chunks(parts, n):
    total = jnp.sum(parts, axis=0)
    body = total[:512].reshape(n, 8, 128)
    tail = total[512:768].reshape(n // 2, 8, 128)
    tail = jnp.concatenate([tail[:, :4], tail[:, 4:]], axis=0)
    gain = jnp.broadcast_to(total[768:].reshape(n, 1, 128), (n, 4, 128))
    return jnp.concatenate([body, tail, gain], axis=1)


def finish_chunk(chunks, scale):
    total = jnp.sum(chunks, axis=0) * scale
    high = total.astype(BF16)
    low = (total - high.astype(F32)).astype(BF16)
    row = lax.broadcasted_iota(jnp.int32, total.shape, 0)
    return jnp.broadcast_to(jnp.where(row == 15, low, high)[None], chunks.shape)


def join_chunks(chunks_ref, rows_ref):
    n, deep = chunks_ref.shape[0], chunks_ref.shape[1] // 2
    half = n // 2
    chunks = chunks_ref[...].astype(F32)
    body = chunks[:, :deep].reshape(512, 128).astype(BF16)
    tail = chunks[:, deep:]
    row = first_rows((half, deep, 128))
    low = jnp.where(row < deep // 2, tail[:half], pltpu.roll(tail[half:], deep // 2, 1))
    low = low.reshape(256, 128).astype(BF16)
    high_gain = tail[:, deep - 2].T[:16]
    low_gain = tail[:, deep - 1].T[:16]
    gain = jnp.concatenate([high_gain, low_gain], axis=1).astype(BF16)
    for k in range(rows_ref.shape[0]):
        rows_ref[k, :512] = body
        rows_ref[k, 512:768] = low
        rows_ref[k, 768:] = gain


def unpack(where_ref, mine_ref, theirs_ref, qkv_ref, proj_ref, up_ref, down_ref, gain_attn_ref, gain_mlp_ref):
    def place(half, rows_ref, gain_ref):
        for piece in range(12):
            k, at = divmod(piece, 3)
            value = rows_ref[k, at * 256 : (at + 1) * 256, :]
            block, right = divmod(piece, 2)
            if half == 1 and block < 4:
                down_ref[block * 256 : (block + 1) * 256, right * 128 : (right + 1) * 128] = value
                continue
            target, column = up_ref, block
            if half == 1:
                target, column = qkv_ref, block - 3
            elif block == 4:
                target, column = proj_ref, 0
            elif block == 5:
                target, column = qkv_ref, 0
            lane = column * 256 + right * 128
            target[:, lane : lane + 128] = value
        lane = lax.broadcasted_iota(jnp.int32, (16, 128), 1)
        for k in range(0, rows_ref.shape[0], 2):
            gain = [rows_ref[k + i, 768:, :].astype(F32) for i in range(2)]
            gain = [g + pltpu.roll(g, 64, 1) for g in gain]
            gain_ref[:, k * 64 : k * 64 + 128] = jnp.where(lane < 64, *gain)[:1]

    @pl.when(where_ref[1] == 0)
    def _():
        place(0, mine_ref, gain_attn_ref)
        place(1, theirs_ref, gain_mlp_ref)

    @pl.when(where_ref[1] == 1)
    def _():
        place(1, mine_ref, gain_mlp_ref)
        place(0, theirs_ref, gain_attn_ref)


def chip_groups(lat_n, lon_n):
    def flat(z, x, y, core):
        return (z * 2 + x // 2) * lon_n + y * 4 + x % 2 * 2 + core

    n_z, n_y = lat_n // 2, lon_n // 4
    over_x = [
        [flat(z, x, y, core) for x in range(4)] for z in range(n_z) for y in range(n_y) for core in range(2)
    ]
    over_yz = [
        [flat(z, x, y, core) for z in range(n_z) for y in range(n_y)] for x in range(4) for core in range(2)
    ]
    return over_x, over_yz


def on_device(
    frame, weight_qkv, weight_proj, gain_attn, weight_up, weight_down, gain_mlp, cotangent
):
    rows, cols, width = frame.shape
    ff = weight_up.shape[1]
    lat_n, lon_n = lax.axis_size("lat"), lax.axis_size("lon")
    tokens = rows * cols
    grad_scale = (tokens * lat_n * lon_n) ** (-0.5)
    across = cols + 2 * EDGE
    dims = {"rows": rows, "cols": cols, "width": width, "ff": ff, "lat_total": rows * lat_n}
    core = lax.axis_index("lon") % 2
    where = jnp.stack([lax.axis_index("lat") * rows, core]).astype(jnp.int32)

    east = [(i, (i + 1) % lon_n) for i in range(lon_n)]
    west = [(j, i) for i, j in east]
    south = [(i, i + 1) for i in range(lat_n - 1)]
    north = [(j, i) for i, j in south]

    from_east = lax.ppermute(frame[:, :EDGE], "lon", west)
    from_west = lax.ppermute(frame[:, cols - EDGE :], "lon", east)
    wide = jnp.concatenate([frame, from_east, from_west], axis=1)
    bottom = lax.ppermute(wide[:RADIUS], "lat", north)
    top = lax.ppermute(wide[rows - RADIUS :], "lat", south)

    weights = (
        weight_qkv,
        weight_proj,
        gain_attn.reshape(1, width),
        weight_up,
        weight_down,
        gain_mlp.reshape(1, width),
    )
    flat = (-1, width)
    block_out, d_mid, dq, up, down, centre, keep, send = local_part(
        where,
        frame.reshape(flat),
        wide.reshape(flat),
        top.reshape(flat),
        bottom.reshape(flat),
        weights,
        cotangent.reshape(flat),
        dims,
    )

    both = ("lat", "lon")
    devices = lat_n * lon_n
    swap = [(i, i ^ 1) for i in range(devices)]
    over_x, over_yz = chip_groups(lat_n, lon_n)
    n_x, n_yz = len(over_x[0]), len(over_yz[0])
    shape = jax.ShapeDtypeStruct

    def exchange(blocks, groups):
        return lax.all_to_all(blocks, both, 0, 0, axis_index_groups=groups)

    up = lax.ppermute(up, "lat", north)
    down = lax.ppermute(down, "lat", south)

    other = lax.ppermute(send, both, swap)
    parts = exchange(keep + other, over_x)

    up = up.reshape(RADIUS, across, 2 * width).astype(F32)
    down = down.reshape(RADIUS, across, 2 * width).astype(F32)
    rest = rows - RADIUS
    centre = centre.reshape(rows, across, 2 * width)
    centre = centre + jnp.pad(up, ((rest, 0), (0, 0), (0, 0))) + jnp.pad(down, ((0, rest), (0, 0), (0, 0)))
    to_east = centre[:, cols : cols + EDGE].astype(BF16)
    to_west = centre[:, cols + EDGE :].astype(BF16)
    from_west = lax.ppermute(to_east, "lon", east)
    from_east = lax.ppermute(to_west, "lon", west)
    chunks = exchange(deal_chunks(parts, n_yz), over_yz)
    chunks, from_west, from_east = lax.optimization_barrier((chunks, from_west, from_east))

    own = exchange(finish_chunk(chunks, grad_scale), over_yz)

    rest = cols - EDGE
    owned = (
        centre[:, :cols]
        + jnp.pad(from_west.astype(F32), ((0, 0), (0, rest), (0, 0)))
        + jnp.pad(from_east.astype(F32), ((0, 0), (rest, 0), (0, 0)))
    )
    d_projected = jnp.concatenate([dq, owned.reshape(tokens, 2 * width).astype(BF16)], axis=1)
    grad_frame = (d_mid + nt(d_projected, weight_qkv)).astype(BF16)

    mine = small_kernel(join_chunks, shape((n_x, 784, 128), BF16), own)
    mine = exchange(mine, over_x)
    theirs = lax.ppermute(mine, both, swap)
    gradients = small_kernel(
        unpack,
        [
            shape((width, 3 * width), BF16),
            shape((width, width), BF16),
            shape((width, ff), BF16),
            shape((ff, width), BF16),
            shape((1, width), F32),
            shape((1, width), F32),
        ],
        where,
        mine,
        theirs,
    )
    gain_sums = [g.reshape(width) for g in gradients[4:]]
    return (
        block_out.reshape(rows, cols, width),
        grad_frame.reshape(rows, cols, width),
        *gradients[:4],
        *gain_sums,
    )


def solution(mesh):
    return jax.shard_map(
        on_device,
        mesh=mesh,
        in_specs=(P("lat", "lon", None), P(), P(), P(), P(), P(), P(), P("lat", "lon", None)),
        out_specs=(P("lat", "lon", None), P("lat", "lon", None), P(), P(), P(), P(), P(), P()),
        check_vma=False,
    )
```

```python
import functools

import jax
import jax.numpy as jnp
from jax import lax
from jax.experimental import pallas as pl
from jax.experimental.pallas import tpu as pltpu
from jax.sharding import PartitionSpec as P


HEADS = 8
RADIUS = 6
EDGE = 8

epsilon = 1e-06
cubic_term = 0.044715
gelu_root = 0.7978845608028654
negative_big = -1e30

F32 = jnp.float32
BF16 = jnp.bfloat16
TOP = 14.0


def nn(left, right):
    return lax.dot_general(left, right, (((1,), (0,)), ((), ())), preferred_element_type=F32)


def nt(left, right):
    return lax.dot_general(left, right, (((1,), (1,)), ((), ())), preferred_element_type=F32)


def gelu_pair(upward):
    tangent = jnp.tanh(gelu_root * (upward + cubic_term * upward * upward * upward))
    activated = 0.5 * upward * (1.0 + tangent)
    derivative = 0.5 * (1.0 + tangent) + 0.5 * upward * (1.0 - tangent * tangent) * gelu_root * (
        1.0 + 3.0 * cubic_term * upward * upward
    )
    return (activated, derivative)


def rms_factor(field):
    return lax.rsqrt(jnp.mean(field * field, axis=-1, keepdims=True) + epsilon)


def norm_backward(incoming, field, factor):
    mean_term = jnp.mean(incoming * field, axis=-1, keepdims=True)
    return factor * (incoming - field * factor * factor * mean_term)


def local_kernel(
    dims,
    where_ref,
    frame_ref,
    wide_ref,
    top_ref,
    bottom_ref,
    wqkv_ref,
    wproj_ref,
    gain_attn_ref,
    wup_ref,
    wdown_ref,
    gain_mlp_ref,
    cot_ref,
    block_out_ref,
    d_mid_ref,
    dq_ref,
    up_ref,
    down_ref,
    centre_ref,
    keep_ref,
    send_ref,
    grads_ref,
    halo,
    keys,
    values,
    keys_t,
    values_t,
    stack_q,
    stack_o,
    bias,
    probs,
    probs_bf,
    d_scores,
    att_t,
    dq_t,
    hidden,
    slope,
    pair_grads,
):
    rows, cols, lat_total = dims["rows"], dims["cols"], dims["lat_total"]
    heads, size, width, ff = HEADS, dims["width"] // HEADS, dims["width"], dims["ff"]
    across = cols + 2 * EDGE
    block_rows = 128 // cols
    blocks = rows // block_rows
    reach = (block_rows + 2 * RADIUS) * across
    step = block_rows * across
    pairs = heads // 2
    head_scale = size ** (-0.5)
    lat_first = where_ref[0]
    core = where_ref[1]
    side = (core, 1 - core)

    def put(index, value):
        half, row = divmod(index, 6)
        grads_ref[side[half], row * 512 : row * 512 + 256, :] = value[:, :128]
        grads_ref[side[half], row * 512 + 256 : row * 512 + 512, :] = value[:, 128:]

    def put_gain(half, terms):
        column = jnp.sum(terms.T, axis=1, keepdims=True)
        grads_ref[side[half], 3072:, :] = jnp.broadcast_to(column, (width, 128))

    rim = RADIUS * across
    inner = rows * across
    halo[0:rim, :] = top_ref[...]
    halo[rim : rim + inner, :] = wide_ref[...]
    halo[rim + inner : inner + 2 * rim, :] = bottom_ref[...]
    grid = halo[...]
    key32 = nn(grid, wqkv_ref[:, width : 2 * width])
    keys[...] = key32.astype(BF16)
    keys_t[...] = key32.T.astype(BF16)
    value32 = nn(grid, wqkv_ref[:, 2 * width :])
    values[...] = value32.astype(BF16)
    values_t[...] = value32.T.astype(BF16)

    lane_head = lax.broadcasted_iota(jnp.int32, (128, width), 1) // size

    def spread(target, field):
        for b in range(blocks):
            part = field[b * 128 : (b + 1) * 128]
            for h in range(heads):
                target[b, h * 128 : (h + 1) * 128, :] = jnp.where(lane_head == h, part, 0.0).astype(BF16)

    own = frame_ref[...]
    spread(stack_q, nn(own, wqkv_ref[:, :width]).astype(BF16).astype(F32))

    at_key = lax.broadcasted_iota(jnp.int32, (reach, 128), 0)
    at_query = lax.broadcasted_iota(jnp.int32, (reach, 128), 1)
    key_row, key_col = at_key // across, at_key % across
    key_col = jnp.where(key_col < cols + EDGE, key_col, key_col - across)
    row_gap = key_row - at_query // cols
    col_gap = key_col - at_query % cols
    near = (row_gap >= 0) & (row_gap <= 2 * RADIUS) & (col_gap >= -RADIUS) & (col_gap <= RADIUS)
    for b in range(blocks):
        row_global = key_row + (lat_first + b * block_rows - RADIUS)
        seen = near & (row_global >= 0) & (row_global < lat_total)
        bias[b] = jnp.where(seen, 0.0, negative_big)

    def diagonal(target, product, b, pair):
        at = pl.multiple_of(pair * 2 * size, 2 * size)
        lane = pl.multiple_of(b * 128, 128)
        target[pl.ds(at, size), pl.ds(lane, 128)] = product[:size, :128]
        target[pl.ds(at + size, size), pl.ds(lane, 128)] = product[size:, 128:]

    def forward(index, _):
        b, pair = index // pairs, index % pairs
        at = pl.multiple_of(pair * 256, 256)
        first = pl.multiple_of(b * step, step)
        rim_bias = bias[b]
        scores = nt(keys[pl.ds(first, reach), :], stack_q[b, pl.ds(at, 256), :]) * head_scale
        scores = scores + jnp.concatenate([rim_bias, rim_bias], axis=1)
        peak = jnp.max(scores, axis=0, keepdims=True)
        expo = jnp.exp(scores - peak)
        total = jnp.sum(expo, axis=0, keepdims=True)
        weight = expo * (1.0 / total)
        probs[index] = weight
        weight_bf = weight.astype(BF16)
        probs_bf[b, :, pl.ds(at, 256)] = weight_bf
        some = values_t[pl.ds(pl.multiple_of(pair * 2 * size, 2 * size), 2 * size), pl.ds(first, reach)]
        diagonal(att_t, nn(some, weight_bf), b, pair)
        return _

    lax.fori_loop(0, blocks * pairs, forward, 0)

    attended_t = att_t[...]
    attended = attended_t.T.astype(BF16)
    proj = nn(attended, wproj_ref[...])
    factor_one = rms_factor(proj)
    mid32 = own.astype(F32) + proj * factor_one * gain_attn_ref[...]
    mid = mid32.astype(BF16)

    downward = jnp.zeros((rows * cols, width), F32)
    for c in range(ff // 256):
        upward = nn(mid, wup_ref[:, c * 256 : (c + 1) * 256])
        activated, derivative = gelu_pair(upward)
        hidden_c = activated.astype(BF16)
        hidden[c] = activated
        slope[c] = derivative
        downward = downward + nn(hidden_c, wdown_ref[c * 256 : (c + 1) * 256, :])
    factor_two = rms_factor(downward)
    block_out_ref[...] = (mid.astype(F32) + downward * factor_two * gain_mlp_ref[...]).astype(BF16)

    incoming = cot_ref[...].astype(F32)
    put_gain(1, incoming * downward * factor_two)
    d_down = norm_backward(incoming * gain_mlp_ref[...], downward, factor_two).astype(BF16)
    mid_t = mid.astype(F32).T.astype(BF16)
    d_mid = incoming
    for c in range(ff // 256):
        d_up = (nt(d_down, wdown_ref[c * 256 : (c + 1) * 256, :]) * slope[c]).astype(BF16)
        d_mid = d_mid + nt(d_up, wup_ref[:, c * 256 : (c + 1) * 256])
        put(c, nn(mid_t, d_up))
        put(6 + c, nn(hidden[c].T.astype(BF16), d_down))
    d_mid_ref[...] = d_mid
    put_gain(0, d_mid * proj * factor_one)
    d_proj = norm_backward(d_mid * gain_attn_ref[...], proj, factor_one).astype(BF16)
    put(4, nn(attended_t.astype(BF16), d_proj))
    spread(stack_o, nt(d_proj, wproj_ref[...]).astype(BF16).astype(F32))

    def backward(index, _):
        b, pair = index // pairs, index % pairs
        at = pl.multiple_of(pair * 256, 256)
        first = pl.multiple_of(b * step, step)
        d_probs = nt(values[pl.ds(first, reach), :], stack_o[b, pl.ds(at, 256), :])
        weight = probs[index]
        d_weighted = jnp.sum(weight * d_probs, axis=0, keepdims=True)
        d_score = (weight * (d_probs - d_weighted) * head_scale).astype(BF16)
        d_scores[b, :, pl.ds(at, 256)] = d_score
        some = keys_t[pl.ds(pl.multiple_of(pair * 2 * size, 2 * size), 2 * size), pl.ds(first, reach)]
        diagonal(dq_t, nn(some, d_score), b, pair)
        return _

    lax.fori_loop(0, blocks * pairs, backward, 0)

    pair_grads[...] = jnp.zeros_like(pair_grads)
    for b in range(blocks):
        pair_grads[b * step : b * step + reach, :width] += nn(d_scores[b], stack_q[b])
        pair_grads[b * step : b * step + reach, width:] += nn(probs_bf[b], stack_o[b])

    dq = dq_t[...].T.astype(BF16)
    dq_ref[...] = dq
    up_ref[...] = pair_grads[0:rim, :].astype(BF16)
    down_ref[...] = pair_grads[rim + inner : inner + 2 * rim, :].astype(BF16)
    centre_ref[...] = pair_grads[rim : rim + inner, :]

    put(5, nn(own.astype(F32).T.astype(BF16), dq))
    grid_t = halo[...].astype(F32).T.astype(BF16)
    for half in range(2):
        terms = pair_grads[:, half * width : (half + 1) * width]
        high = terms.astype(BF16)
        low = (terms - high.astype(F32)).astype(BF16)
        put(10 + half, nn(grid_t, high) + nn(grid_t, low))
    keep_ref[...] = grads_ref[0]
    send_ref[...] = grads_ref[1]


def local_part(where, frame, wide, top, bottom, weights, cotangent, dims):
    rows, cols, width, ff = dims["rows"], dims["cols"], dims["width"], dims["ff"]
    across = cols + 2 * EDGE
    grid = (rows + 2 * RADIUS) * across
    rim = RADIUS * across
    block_rows = 128 // cols
    blocks = rows // block_rows
    reach = (block_rows + 2 * RADIUS) * across
    tokens = rows * cols
    pairs = HEADS // 2
    shape = jax.ShapeDtypeStruct
    vmem = pl.BlockSpec(memory_space=pltpu.VMEM)
    outs = [
        shape((tokens, width), BF16),
        shape((tokens, width), F32),
        shape((tokens, width), BF16),
        shape((rim, 2 * width), BF16),
        shape((rim, 2 * width), BF16),
        shape((rows * across, 2 * width), F32),
        shape((3072 + width, 128), F32),
        shape((3072 + width, 128), F32),
    ]
    return pl.pallas_call(
        functools.partial(local_kernel, dims),
        out_shape=outs,
        in_specs=[pl.BlockSpec(memory_space=pltpu.SMEM)] + [vmem] * 11,
        out_specs=[vmem] * len(outs),
        scratch_shapes=[
            pltpu.VMEM((2, 3072 + width, 128), F32),
            pltpu.VMEM((grid, width), BF16),
            pltpu.VMEM((grid, width), BF16),
            pltpu.VMEM((grid, width), BF16),
            pltpu.VMEM((width, grid), BF16),
            pltpu.VMEM((width, grid), BF16),
            pltpu.VMEM((blocks, HEADS * 128, width), BF16),
            pltpu.VMEM((blocks, HEADS * 128, width), BF16),
            pltpu.VMEM((blocks, reach, 128), F32),
            pltpu.VMEM((blocks * pairs, reach, 256), F32),
            pltpu.VMEM((blocks, reach, HEADS * 128), BF16),
            pltpu.VMEM((blocks, reach, HEADS * 128), BF16),
            pltpu.VMEM((width, tokens), F32),
            pltpu.VMEM((width, tokens), F32),
            pltpu.VMEM((ff // 256, tokens, 256), F32),
            pltpu.VMEM((ff // 256, tokens, 256), F32),
            pltpu.VMEM((grid, 2 * width), F32),
        ],
        name="local_part",
    )(where, frame, wide, top, bottom, *weights, cotangent)


def small_kernel(body, outs, *args, scratch=()):
    vmem = pl.BlockSpec(memory_space=pltpu.VMEM)
    smem = pl.BlockSpec(memory_space=pltpu.SMEM)
    return pl.pallas_call(
        body,
        out_shape=outs,
        in_specs=[smem if a.dtype == jnp.int32 else vmem for a in args],
        out_specs=jax.tree.map(lambda _: vmem, outs),
        scratch_shapes=scratch,
    )(*args)


def first_rows(shape):
    return lax.broadcasted_iota(jnp.int32, shape, 1)


def scales(largest):
    power = jnp.clip(jnp.ceil(jnp.log2(jnp.maximum(largest, 1e-37))), -100.0, 127.0)
    return power, jnp.exp2(TOP - power)


def pick(table, i):
    return jnp.broadcast_to(table[:, i : i + 1], (8, 128))


def note(largest, i, value):
    value = jnp.max(jnp.max(jnp.abs(value).reshape(-1, 8, 128), axis=0), keepdims=True)
    lane = lax.broadcasted_iota(jnp.int32, (8, 128), 1)
    return jnp.where(lane == i, value, largest)


def pack_x(keep_ref, other_ref, parts_ref, sum_ref):
    blocks = sum_ref.shape[0] // 256
    largest = jnp.zeros((8, 128), F32)
    for i in range(blocks):
        at = i * 256
        value = keep_ref[at : at + 256, :] + other_ref[at : at + 256, :]
        sum_ref[at : at + 256, :] = value
        largest = note(largest, i, value)
    power, factor = scales(largest)
    row = lax.broadcasted_iota(jnp.int32, (8, 128), 0)
    last = blocks - 1
    gain_factor = pick(factor, last)
    for k in range(4):
        powers = pick(power, last)
        for i in range(3):
            at = (3 * k + i) * 256
            value = sum_ref[at : at + 256, :].reshape(32, 8, 128) * pick(factor, 3 * k + i)
            parts_ref[k, i * 256 : (i + 1) * 256, :] = value.reshape(256, 128)
            powers = jnp.where(row == i, pick(power, 3 * k + i), powers)
        at = last * 256 + k * 64
        parts_ref[k, 768:832, :] = (sum_ref[at : at + 64, :].reshape(8, 8, 128) * gain_factor).reshape(64, 128)
        parts_ref[k, 832:, :] = powers


def pack_chunks(parts_ref, chunks_ref, sum_ref):
    n = chunks_ref.shape[0]
    half = n // 2
    scale = [jnp.exp2(parts_ref[x, 832:, :] - TOP) for x in range(4)]
    largest = jnp.zeros((8, 128), F32)
    for i, (at, size) in enumerate(((0, 256), (256, 256), (512, 256), (768, 64))):
        total = parts_ref[0, at : at + size, :] * scale[0][i : i + 1]
        for x in range(1, 4):
            total = total + parts_ref[x, at : at + size, :] * scale[x][i : i + 1]
        sum_ref[at : at + size, :] = total
        largest = note(largest, i, total)
    power, factor = scales(largest)

    def scaled(i):
        return sum_ref[i * 256 : (i + 1) * 256, :].reshape(half, 8, 128) * pick(factor, i)

    gain = (sum_ref[768:, :] * pick(factor, 3)[:1]).reshape(n, 1, 128)
    row = lax.broadcasted_iota(jnp.int32, (8, 128), 0)
    tail = scaled(2)
    for i in range(2):
        to = i * half
        chunks_ref[to : to + half, :8] = scaled(i)
        powers = jnp.where(row == 5, pick(power, i), pick(power, 2))
        powers = jnp.where(row == 7, pick(power, 3), powers)
        piece = tail if i == 0 else pltpu.roll(tail, 4, 1)
        piece = jnp.where(row < 4, piece, gain[to : to + half])
        chunks_ref[to : to + half, 8:] = jnp.where(row > 4, powers, piece)


def finish_chunk(scale, chunks_ref, own_ref):
    body = chunks_ref[:, :8]
    tail = chunks_ref[:, 8:]
    factor = jnp.exp2(tail - TOP)
    body = jnp.sum(body * factor[:, 5:6], axis=0)
    row = lax.broadcasted_iota(jnp.int32, tail.shape, 1)
    factor = jnp.where(row < 4, factor[:, 6:7], factor[:, 7:8])
    tail = jnp.sum(jnp.where(row < 5, tail * factor, 0.0), axis=0) * scale
    gain = tail[4:5]
    high = gain.astype(BF16).astype(F32)
    row = lax.broadcasted_iota(jnp.int32, tail.shape, 0)
    tail = jnp.where(row == 6, high, jnp.where(row == 7, gain - high, tail))
    total = jnp.concatenate([body * scale, tail], axis=0).astype(BF16)
    own_ref[...] = jnp.broadcast_to(total[None], own_ref.shape)


def join_chunks(chunks_ref, rows_ref):
    n, deep = chunks_ref.shape[0], chunks_ref.shape[1] // 2
    half = n // 2
    chunks = chunks_ref[...].astype(F32)
    body = chunks[:, :deep].reshape(512, 128).astype(BF16)
    tail = chunks[:, deep:]
    row = first_rows((half, deep, 128))
    low = jnp.where(row < deep // 2, tail[:half], pltpu.roll(tail[half:], deep // 2, 1))
    low = low.reshape(256, 128).astype(BF16)
    high_gain = tail[:, deep - 2].T[:16]
    low_gain = tail[:, deep - 1].T[:16]
    gain = jnp.concatenate([high_gain, low_gain], axis=1).astype(BF16)
    for k in range(rows_ref.shape[0]):
        rows_ref[k, :512] = body
        rows_ref[k, 512:768] = low
        rows_ref[k, 768:] = gain


def unpack(where_ref, mine_ref, theirs_ref, qkv_ref, proj_ref, up_ref, down_ref, gain_attn_ref, gain_mlp_ref):
    def place(half, rows_ref, gain_ref):
        for piece in range(12):
            k, at = divmod(piece, 3)
            value = rows_ref[k, at * 256 : (at + 1) * 256, :]
            block, right = divmod(piece, 2)
            if half == 1 and block < 4:
                down_ref[block * 256 : (block + 1) * 256, right * 128 : (right + 1) * 128] = value
                continue
            target, column = up_ref, block
            if half == 1:
                target, column = qkv_ref, block - 3
            elif block == 4:
                target, column = proj_ref, 0
            elif block == 5:
                target, column = qkv_ref, 0
            lane = column * 256 + right * 128
            target[:, lane : lane + 128] = value
        lane = lax.broadcasted_iota(jnp.int32, (16, 128), 1)
        for k in range(0, rows_ref.shape[0], 2):
            gain = [rows_ref[k + i, 768:, :].astype(F32) for i in range(2)]
            gain = [g + pltpu.roll(g, 64, 1) for g in gain]
            gain_ref[:, k * 64 : k * 64 + 128] = jnp.where(lane < 64, *gain)[:1]

    @pl.when(where_ref[1] == 0)
    def _():
        place(0, mine_ref, gain_attn_ref)
        place(1, theirs_ref, gain_mlp_ref)

    @pl.when(where_ref[1] == 1)
    def _():
        place(1, mine_ref, gain_mlp_ref)
        place(0, theirs_ref, gain_attn_ref)


def chip_groups(lat_n, lon_n):
    def flat(z, x, y, core):
        return (z * 2 + x // 2) * lon_n + y * 4 + x % 2 * 2 + core

    n_z, n_y = lat_n // 2, lon_n // 4
    over_x = [
        [flat(z, x, y, core) for x in range(4)] for z in range(n_z) for y in range(n_y) for core in range(2)
    ]
    over_yz = [
        [flat(z, x, y, core) for z in range(n_z) for y in range(n_y)] for x in range(4) for core in range(2)
    ]
    return over_x, over_yz


def on_device(
    frame, weight_qkv, weight_proj, gain_attn, weight_up, weight_down, gain_mlp, cotangent
):
    rows, cols, width = frame.shape
    ff = weight_up.shape[1]
    lat_n, lon_n = lax.axis_size("lat"), lax.axis_size("lon")
    tokens = rows * cols
    grad_scale = (tokens * lat_n * lon_n) ** (-0.5)
    across = cols + 2 * EDGE
    dims = {"rows": rows, "cols": cols, "width": width, "ff": ff, "lat_total": rows * lat_n}
    core = lax.axis_index("lon") % 2
    where = jnp.stack([lax.axis_index("lat") * rows, core]).astype(jnp.int32)

    east = [(i, (i + 1) % lon_n) for i in range(lon_n)]
    west = [(j, i) for i, j in east]
    south = [(i, i + 1) for i in range(lat_n - 1)]
    north = [(j, i) for i, j in south]

    from_east = lax.ppermute(frame[:, :EDGE], "lon", west)
    from_west = lax.ppermute(frame[:, cols - EDGE :], "lon", east)
    wide = jnp.concatenate([frame, from_east, from_west], axis=1)
    bottom = lax.ppermute(wide[:RADIUS], "lat", north)
    top = lax.ppermute(wide[rows - RADIUS :], "lat", south)

    weights = (
        weight_qkv,
        weight_proj,
        gain_attn.reshape(1, width),
        weight_up,
        weight_down,
        gain_mlp.reshape(1, width),
    )
    flat = (-1, width)
    block_out, d_mid, dq, up, down, centre, keep, send = local_part(
        where,
        frame.reshape(flat),
        wide.reshape(flat),
        top.reshape(flat),
        bottom.reshape(flat),
        weights,
        cotangent.reshape(flat),
        dims,
    )

    both = ("lat", "lon")
    devices = lat_n * lon_n
    swap = [(i, i ^ 1) for i in range(devices)]
    over_x, over_yz = chip_groups(lat_n, lon_n)
    n_x, n_yz = len(over_x[0]), len(over_yz[0])
    shape = jax.ShapeDtypeStruct

    def exchange(blocks, groups):
        return lax.all_to_all(blocks, both, 0, 0, axis_index_groups=groups)

    up = lax.ppermute(up, "lat", north)
    down = lax.ppermute(down, "lat", south)

    other = lax.ppermute(send, both, swap)
    parts = small_kernel(pack_x, shape((n_x, 840, 128), F32), keep, other, scratch=[pltpu.VMEM(keep.shape, F32)])
    parts = exchange(parts.astype(jnp.float16), over_x)
    chunks = small_kernel(
        pack_chunks, shape((n_yz, 16, 128), F32), parts.astype(F32), scratch=[pltpu.VMEM((832, 128), F32)]
    )
    chunks = exchange(chunks.astype(jnp.float16), over_yz)

    up = up.reshape(RADIUS, across, 2 * width).astype(F32)
    down = down.reshape(RADIUS, across, 2 * width).astype(F32)
    rest = rows - RADIUS
    centre = centre.reshape(rows, across, 2 * width)
    centre = centre + jnp.pad(up, ((rest, 0), (0, 0), (0, 0))) + jnp.pad(down, ((0, rest), (0, 0), (0, 0)))
    to_east = centre[:, cols : cols + EDGE].astype(BF16)
    to_west = centre[:, cols + EDGE :].astype(BF16)
    from_west = lax.ppermute(to_east, "lon", east)
    from_east = lax.ppermute(to_west, "lon", west)

    own = small_kernel(functools.partial(finish_chunk, grad_scale), shape((n_yz, 16, 128), BF16), chunks.astype(F32))
    own = exchange(own, over_yz)
    own, from_west, from_east = lax.optimization_barrier((own, from_west, from_east))

    rest = cols - EDGE
    owned = (
        centre[:, :cols]
        + jnp.pad(from_west.astype(F32), ((0, 0), (0, rest), (0, 0)))
        + jnp.pad(from_east.astype(F32), ((0, 0), (rest, 0), (0, 0)))
    )
    d_projected = jnp.concatenate([dq, owned.reshape(tokens, 2 * width).astype(BF16)], axis=1)
    grad_frame = (d_mid + nt(d_projected, weight_qkv)).astype(BF16)

    mine = small_kernel(join_chunks, shape((n_x, 784, 128), BF16), own)
    mine = exchange(mine, over_x)
    theirs = lax.ppermute(mine, both, swap)
    gradients = small_kernel(
        unpack,
        [
            shape((width, 3 * width), BF16),
            shape((width, width), BF16),
            shape((width, ff), BF16),
            shape((ff, width), BF16),
            shape((1, width), F32),
            shape((1, width), F32),
        ],
        where,
        mine,
        theirs,
    )
    gain_sums = [g.reshape(width) for g in gradients[4:]]
    return (
        block_out.reshape(rows, cols, width),
        grad_frame.reshape(rows, cols, width),
        *gradients[:4],
        *gain_sums,
    )


def solution(mesh):
    return jax.shard_map(
        on_device,
        mesh=mesh,
        in_specs=(P("lat", "lon", None), P(), P(), P(), P(), P(), P(), P("lat", "lon", None)),
        out_specs=(P("lat", "lon", None), P("lat", "lon", None), P(), P(), P(), P(), P(), P()),
        check_vma=False,
    )
```

```python
import functools

import jax
import jax.numpy as jnp
from jax import lax
from jax.experimental import pallas as pl
from jax.experimental.pallas import tpu as pltpu
from jax.sharding import PartitionSpec as P

HEADS = 8
RADIUS = 6
EDGE = 8

epsilon = 1e-06
cubic_term = 0.044715
gelu_root = 0.7978845608028654
negative_big = -1e30

F32 = jnp.float32
BF16 = jnp.bfloat16
TOP = 14.0


def nn(left, right):
    return lax.dot_general(left, right, (((1,), (0,)), ((), ())), preferred_element_type=F32)


def nt(left, right):
    return lax.dot_general(left, right, (((1,), (1,)), ((), ())), preferred_element_type=F32)


def gelu_pair(upward):
    tangent = jnp.tanh(gelu_root * (upward + cubic_term * upward * upward * upward))
    activated = 0.5 * upward * (1.0 + tangent)
    derivative = 0.5 * (1.0 + tangent) + 0.5 * upward * (1.0 - tangent * tangent) * gelu_root * (
        1.0 + 3.0 * cubic_term * upward * upward
    )
    return (activated, derivative)


def rms_factor(field):
    return lax.rsqrt(jnp.mean(field * field, axis=-1, keepdims=True) + epsilon)


def norm_backward(incoming, field, factor):
    mean_term = jnp.mean(incoming * field, axis=-1, keepdims=True)
    return factor * (incoming - field * factor * factor * mean_term)


def local_kernel(
    dims,
    where_ref,
    frame_ref,
    wide_ref,
    top_ref,
    bottom_ref,
    wqkv_ref,
    wproj_ref,
    gain_attn_ref,
    wup_ref,
    wdown_ref,
    gain_mlp_ref,
    cot_ref,
    block_out_ref,
    d_mid_ref,
    dq_ref,
    up_ref,
    down_ref,
    centre_ref,
    keep_ref,
    send_ref,
    grads_ref,
    halo,
    keys,
    values,
    keys_t,
    values_t,
    stack_q,
    stack_o,
    bias,
    probs,
    probs_bf,
    d_scores,
    att_t,
    dq_t,
    hidden,
    slope,
    pair_grads,
):
    rows, cols, lat_total = dims["rows"], dims["cols"], dims["lat_total"]
    heads, size, width, ff = HEADS, dims["width"] // HEADS, dims["width"], dims["ff"]
    across = cols + 2 * EDGE
    block_rows = 128 // cols
    blocks = rows // block_rows
    reach = (block_rows + 2 * RADIUS) * across
    step = block_rows * across
    pairs = heads // 2
    head_scale = size ** (-0.5)
    lat_first = where_ref[0]
    core = where_ref[1]
    side = (core, 1 - core)

    def put(index, value):
        half, row = divmod(index, 6)
        grads_ref[side[half], row * 512 : row * 512 + 256, :] = value[:, :128]
        grads_ref[side[half], row * 512 + 256 : row * 512 + 512, :] = value[:, 128:]

    def put_gain(half, terms):
        column = jnp.sum(terms.T, axis=1, keepdims=True)
        grads_ref[side[half], 3072:, :] = jnp.broadcast_to(column, (width, 128))

    rim = RADIUS * across
    inner = rows * across
    halo[0:rim, :] = top_ref[...]
    halo[rim : rim + inner, :] = wide_ref[...]
    halo[rim + inner : inner + 2 * rim, :] = bottom_ref[...]
    grid = halo[...]
    key32 = nn(grid, wqkv_ref[:, width : 2 * width])
    keys[...] = key32.astype(BF16)
    keys_t[...] = key32.T.astype(BF16)
    value32 = nn(grid, wqkv_ref[:, 2 * width :])
    values[...] = value32.astype(BF16)
    values_t[...] = value32.T.astype(BF16)

    lane_head = lax.broadcasted_iota(jnp.int32, (128, width), 1) // size

    def spread(target, field):
        for b in range(blocks):
            part = field[b * 128 : (b + 1) * 128]
            for h in range(heads):
                target[b, h * 128 : (h + 1) * 128, :] = jnp.where(lane_head == h, part, 0.0).astype(BF16)

    own = frame_ref[...]
    spread(stack_q, nn(own, wqkv_ref[:, :width]).astype(BF16).astype(F32))

    at_key = lax.broadcasted_iota(jnp.int32, (reach, 128), 0)
    at_query = lax.broadcasted_iota(jnp.int32, (reach, 128), 1)
    key_row, key_col = at_key // across, at_key % across
    key_col = jnp.where(key_col < cols + EDGE, key_col, key_col - across)
    row_gap = key_row - at_query // cols
    col_gap = key_col - at_query % cols
    near = (row_gap >= 0) & (row_gap <= 2 * RADIUS) & (col_gap >= -RADIUS) & (col_gap <= RADIUS)
    for b in range(blocks):
        row_global = key_row + (lat_first + b * block_rows - RADIUS)
        seen = near & (row_global >= 0) & (row_global < lat_total)
        bias[b] = jnp.where(seen, 0.0, negative_big)

    def diagonal(target, product, b, pair):
        at = pl.multiple_of(pair * 2 * size, 2 * size)
        lane = pl.multiple_of(b * 128, 128)
        target[pl.ds(at, size), pl.ds(lane, 128)] = product[:size, :128]
        target[pl.ds(at + size, size), pl.ds(lane, 128)] = product[size:, 128:]

    def forward(index, _):
        b, pair = index // pairs, index % pairs
        at = pl.multiple_of(pair * 256, 256)
        first = pl.multiple_of(b * step, step)
        rim_bias = bias[b]
        scores = nt(keys[pl.ds(first, reach), :], stack_q[b, pl.ds(at, 256), :]) * head_scale
        scores = scores + jnp.concatenate([rim_bias, rim_bias], axis=1)
        peak = jnp.max(scores, axis=0, keepdims=True)
        expo = jnp.exp(scores - peak)
        total = jnp.sum(expo, axis=0, keepdims=True)
        weight = expo * (1.0 / total)
        probs[index] = weight
        weight_bf = weight.astype(BF16)
        probs_bf[b, :, pl.ds(at, 256)] = weight_bf
        some = values_t[pl.ds(pl.multiple_of(pair * 2 * size, 2 * size), 2 * size), pl.ds(first, reach)]
        diagonal(att_t, nn(some, weight_bf), b, pair)
        return _

    lax.fori_loop(0, blocks * pairs, forward, 0)

    attended_t = att_t[...]
    attended = attended_t.T.astype(BF16)
    proj = nn(attended, wproj_ref[...])
    factor_one = rms_factor(proj)
    mid32 = own.astype(F32) + proj * factor_one * gain_attn_ref[...]
    mid = mid32.astype(BF16)

    downward = jnp.zeros((rows * cols, width), F32)
    for c in range(ff // 256):
        upward = nn(mid, wup_ref[:, c * 256 : (c + 1) * 256])
        activated, derivative = gelu_pair(upward)
        hidden_c = activated.astype(BF16)
        hidden[c] = activated
        slope[c] = derivative
        downward = downward + nn(hidden_c, wdown_ref[c * 256 : (c + 1) * 256, :])
    factor_two = rms_factor(downward)
    block_out_ref[...] = (mid.astype(F32) + downward * factor_two * gain_mlp_ref[...]).astype(BF16)

    incoming = cot_ref[...].astype(F32)
    put_gain(1, incoming * downward * factor_two)
    d_down = norm_backward(incoming * gain_mlp_ref[...], downward, factor_two).astype(BF16)
    mid_t = mid.astype(F32).T.astype(BF16)
    d_mid = incoming
    for c in range(ff // 256):
        d_up = (nt(d_down, wdown_ref[c * 256 : (c + 1) * 256, :]) * slope[c]).astype(BF16)
        d_mid = d_mid + nt(d_up, wup_ref[:, c * 256 : (c + 1) * 256])
        put(c, nn(mid_t, d_up))
        put(6 + c, nn(hidden[c].T.astype(BF16), d_down))
    d_mid_ref[...] = d_mid
    put_gain(0, d_mid * proj * factor_one)
    d_proj = norm_backward(d_mid * gain_attn_ref[...], proj, factor_one).astype(BF16)
    put(4, nn(attended_t.astype(BF16), d_proj))
    spread(stack_o, nt(d_proj, wproj_ref[...]).astype(BF16).astype(F32))

    def backward(index, _):
        b, pair = index // pairs, index % pairs
        at = pl.multiple_of(pair * 256, 256)
        first = pl.multiple_of(b * step, step)
        d_probs = nt(values[pl.ds(first, reach), :], stack_o[b, pl.ds(at, 256), :])
        weight = probs[index]
        d_weighted = jnp.sum(weight * d_probs, axis=0, keepdims=True)
        d_score = (weight * (d_probs - d_weighted) * head_scale).astype(BF16)
        d_scores[b, :, pl.ds(at, 256)] = d_score
        some = keys_t[pl.ds(pl.multiple_of(pair * 2 * size, 2 * size), 2 * size), pl.ds(first, reach)]
        diagonal(dq_t, nn(some, d_score), b, pair)
        return _

    lax.fori_loop(0, blocks * pairs, backward, 0)

    pair_grads[...] = jnp.zeros_like(pair_grads)
    for b in range(blocks):
        pair_grads[b * step : b * step + reach, :width] += nn(d_scores[b], stack_q[b])
        pair_grads[b * step : b * step + reach, width:] += nn(probs_bf[b], stack_o[b])

    dq = dq_t[...].T.astype(BF16)
    dq_ref[...] = dq
    up_ref[...] = pair_grads[0:rim, :].astype(BF16)
    down_ref[...] = pair_grads[rim + inner : inner + 2 * rim, :].astype(BF16)
    centre_ref[...] = pair_grads[rim : rim + inner, :]

    put(5, nn(own.astype(F32).T.astype(BF16), dq))
    grid_t = halo[...].astype(F32).T.astype(BF16)
    for half in range(2):
        terms = pair_grads[:, half * width : (half + 1) * width]
        high = terms.astype(BF16)
        low = (terms - high.astype(F32)).astype(BF16)
        put(10 + half, nn(grid_t, high) + nn(grid_t, low))
    keep_ref[...] = grads_ref[0]
    send_ref[...] = grads_ref[1]


def local_part(where, frame, wide, top, bottom, weights, cotangent, dims):
    rows, cols, width, ff = dims["rows"], dims["cols"], dims["width"], dims["ff"]
    across = cols + 2 * EDGE
    grid = (rows + 2 * RADIUS) * across
    rim = RADIUS * across
    block_rows = 128 // cols
    blocks = rows // block_rows
    reach = (block_rows + 2 * RADIUS) * across
    tokens = rows * cols
    pairs = HEADS // 2
    shape = jax.ShapeDtypeStruct
    vmem = pl.BlockSpec(memory_space=pltpu.VMEM)
    outs = [
        shape((tokens, width), BF16),
        shape((tokens, width), F32),
        shape((tokens, width), BF16),
        shape((rim, 2 * width), BF16),
        shape((rim, 2 * width), BF16),
        shape((rows * across, 2 * width), F32),
        shape((3072 + width, 128), F32),
        shape((3072 + width, 128), F32),
    ]
    return pl.pallas_call(
        functools.partial(local_kernel, dims),
        out_shape=outs,
        in_specs=[pl.BlockSpec(memory_space=pltpu.SMEM)] + [vmem] * 11,
        out_specs=[vmem] * len(outs),
        scratch_shapes=[
            pltpu.VMEM((2, 3072 + width, 128), F32),
            pltpu.VMEM((grid, width), BF16),
            pltpu.VMEM((grid, width), BF16),
            pltpu.VMEM((grid, width), BF16),
            pltpu.VMEM((width, grid), BF16),
            pltpu.VMEM((width, grid), BF16),
            pltpu.VMEM((blocks, HEADS * 128, width), BF16),
            pltpu.VMEM((blocks, HEADS * 128, width), BF16),
            pltpu.VMEM((blocks, reach, 128), F32),
            pltpu.VMEM((blocks * pairs, reach, 256), F32),
            pltpu.VMEM((blocks, reach, HEADS * 128), BF16),
            pltpu.VMEM((blocks, reach, HEADS * 128), BF16),
            pltpu.VMEM((width, tokens), F32),
            pltpu.VMEM((width, tokens), F32),
            pltpu.VMEM((ff // 256, tokens, 256), F32),
            pltpu.VMEM((ff // 256, tokens, 256), F32),
            pltpu.VMEM((grid, 2 * width), F32),
        ],
        name="local_part",
    )(where, frame, wide, top, bottom, *weights, cotangent)


def small_kernel(body, outs, *args, scratch=()):
    vmem = pl.BlockSpec(memory_space=pltpu.VMEM)
    smem = pl.BlockSpec(memory_space=pltpu.SMEM)
    return pl.pallas_call(
        body,
        out_shape=outs,
        in_specs=[smem if a.dtype == jnp.int32 else vmem for a in args],
        out_specs=jax.tree.map(lambda _: vmem, outs),
        scratch_shapes=scratch,
    )(*args)


def first_rows(shape):
    return lax.broadcasted_iota(jnp.int32, shape, 1)


def pack_chunks(keep_ref, other_ref, chunks_ref, sum_ref):
    n = chunks_ref.shape[0] // 4
    half = n // 2
    blocks = sum_ref.shape[0] // 256
    column = lax.broadcasted_iota(jnp.int32, (8, 128), 1)
    largest = jnp.zeros((8, 128), F32)
    for i in range(blocks):
        at = i * 256
        value = keep_ref[at : at + 256, :] + other_ref[at : at + 256, :]
        sum_ref[at : at + 256, :] = value
        value = jnp.max(jnp.max(jnp.abs(value).reshape(32, 8, 128), axis=0), keepdims=True)
        largest = jnp.where(column == i, value, largest)
    power = jnp.clip(jnp.ceil(jnp.log2(jnp.maximum(largest, 1e-37))), -100.0, 127.0)
    factor = jnp.exp2(TOP - power)

    def pick(table, i):
        return jnp.broadcast_to(table[:, i : i + 1], (8, 128))

    def scaled(i):
        return sum_ref[i * 256 : (i + 1) * 256, :].reshape(half, 8, 128) * pick(factor, i)

    gain = (sum_ref[3072:, :] * pick(factor, 12)[:1]).reshape(4, n, 1, 128)
    row = lax.broadcasted_iota(jnp.int32, (8, 128), 0)
    for k in range(4):
        tail = scaled(3 * k + 2)
        for i in range(2):
            to = k * n + i * half
            chunks_ref[to : to + half, :8] = scaled(3 * k + i)
            powers = jnp.where(row == 5, pick(power, 3 * k + i), pick(power, 3 * k + 2))
            powers = jnp.where(row == 7, pick(power, 12), powers)
            piece = tail if i == 0 else pltpu.roll(tail, 4, 1)
            piece = jnp.where(row < 4, piece, gain[k, i * half : (i + 1) * half])
            chunks_ref[to : to + half, 8:] = jnp.where(row > 4, powers, piece)


def finish_chunk(scale, chunks_ref, own_ref):
    body = chunks_ref[:, :8]
    tail = chunks_ref[:, 8:]
    factor = jnp.exp2(tail - TOP)
    body = jnp.sum(body * factor[:, 5:6], axis=0)
    row = lax.broadcasted_iota(jnp.int32, tail.shape, 1)
    factor = jnp.where(row < 4, factor[:, 6:7], factor[:, 7:8])
    tail = jnp.sum(jnp.where(row < 5, tail * factor, 0.0), axis=0) * scale
    gain = tail[4:5]
    high = gain.astype(BF16).astype(F32)
    row = lax.broadcasted_iota(jnp.int32, tail.shape, 0)
    tail = jnp.where(row == 6, high, jnp.where(row == 7, gain - high, tail))
    total = jnp.concatenate([body * scale, tail], axis=0).astype(BF16)
    own_ref[...] = jnp.broadcast_to(total[None], own_ref.shape)


def join_chunks(chunks_ref, rows_ref):
    n, deep = chunks_ref.shape[0], chunks_ref.shape[1] // 2
    half = n // 2
    chunks = chunks_ref[...].astype(F32)
    body = chunks[:, :deep].reshape(512, 128).astype(BF16)
    tail = chunks[:, deep:]
    row = first_rows((half, deep, 128))
    low = jnp.where(row < deep // 2, tail[:half], pltpu.roll(tail[half:], deep // 2, 1))
    low = low.reshape(256, 128).astype(BF16)
    high_gain = tail[:, deep - 2].T[:16]
    low_gain = tail[:, deep - 1].T[:16]
    gain = jnp.concatenate([high_gain, low_gain], axis=1).astype(BF16)
    for k in range(rows_ref.shape[0]):
        rows_ref[k, :512] = body
        rows_ref[k, 512:768] = low
        rows_ref[k, 768:] = gain


def unpack(where_ref, mine_ref, theirs_ref, qkv_ref, proj_ref, up_ref, down_ref, gain_attn_ref, gain_mlp_ref):
    def place(half, rows_ref, gain_ref):
        for piece in range(12):
            k, at = divmod(piece, 3)
            value = rows_ref[k, at * 256 : (at + 1) * 256, :]
            block, right = divmod(piece, 2)
            if half == 1 and block < 4:
                down_ref[block * 256 : (block + 1) * 256, right * 128 : (right + 1) * 128] = value
                continue
            target, column = up_ref, block
            if half == 1:
                target, column = qkv_ref, block - 3
            elif block == 4:
                target, column = proj_ref, 0
            elif block == 5:
                target, column = qkv_ref, 0
            lane = column * 256 + right * 128
            target[:, lane : lane + 128] = value
        lane = lax.broadcasted_iota(jnp.int32, (16, 128), 1)
        for k in range(0, rows_ref.shape[0], 2):
            gain = [rows_ref[k + i, 768:, :].astype(F32) for i in range(2)]
            gain = [g + pltpu.roll(g, 64, 1) for g in gain]
            gain_ref[:, k * 64 : k * 64 + 128] = jnp.where(lane < 64, *gain)[:1]

    @pl.when(where_ref[1] == 0)
    def _():
        place(0, mine_ref, gain_attn_ref)
        place(1, theirs_ref, gain_mlp_ref)

    @pl.when(where_ref[1] == 1)
    def _():
        place(1, mine_ref, gain_mlp_ref)
        place(0, theirs_ref, gain_attn_ref)


def chip_groups(lat_n, lon_n):
    def flat(z, x, y, core):
        return (z * 2 + x // 2) * lon_n + y * 4 + x % 2 * 2 + core

    n_z, n_y = lat_n // 2, lon_n // 4
    over_x = [
        [flat(z, x, y, core) for x in range(4)] for z in range(n_z) for y in range(n_y) for core in range(2)
    ]
    over_yz = [
        [flat(z, x, y, core) for z in range(n_z) for y in range(n_y)] for x in range(4) for core in range(2)
    ]
    over_chips = [
        [flat(z, x, y, core) for x in range(4) for z in range(n_z) for y in range(n_y)] for core in range(2)
    ]
    return over_x, over_yz, over_chips


def on_device(
    frame, weight_qkv, weight_proj, gain_attn, weight_up, weight_down, gain_mlp, cotangent
):
    rows, cols, width = frame.shape
    ff = weight_up.shape[1]
    lat_n, lon_n = lax.axis_size("lat"), lax.axis_size("lon")
    tokens = rows * cols
    grad_scale = (tokens * lat_n * lon_n) ** (-0.5)
    across = cols + 2 * EDGE
    dims = {"rows": rows, "cols": cols, "width": width, "ff": ff, "lat_total": rows * lat_n}
    core = lax.axis_index("lon") % 2
    where = jnp.stack([lax.axis_index("lat") * rows, core]).astype(jnp.int32)

    east = [(i, (i + 1) % lon_n) for i in range(lon_n)]
    west = [(j, i) for i, j in east]
    south = [(i, i + 1) for i in range(lat_n - 1)]
    north = [(j, i) for i, j in south]

    from_east = lax.ppermute(frame[:, :EDGE], "lon", west)
    from_west = lax.ppermute(frame[:, cols - EDGE :], "lon", east)
    wide = jnp.concatenate([frame, from_east, from_west], axis=1)
    bottom = lax.ppermute(wide[:RADIUS], "lat", north)
    top = lax.ppermute(wide[rows - RADIUS :], "lat", south)

    weights = (
        weight_qkv,
        weight_proj,
        gain_attn.reshape(1, width),
        weight_up,
        weight_down,
        gain_mlp.reshape(1, width),
    )
    flat = (-1, width)
    block_out, d_mid, dq, up, down, centre, keep, send = local_part(
        where,
        frame.reshape(flat),
        wide.reshape(flat),
        top.reshape(flat),
        bottom.reshape(flat),
        weights,
        cotangent.reshape(flat),
        dims,
    )

    both = ("lat", "lon")
    devices = lat_n * lon_n
    swap = [(i, i ^ 1) for i in range(devices)]
    over_x, over_yz, over_chips = chip_groups(lat_n, lon_n)
    n_x, n_yz = len(over_x[0]), len(over_yz[0])
    shape = jax.ShapeDtypeStruct

    def exchange(blocks, groups):
        return lax.all_to_all(blocks, both, 0, 0, axis_index_groups=groups)

    up = lax.ppermute(up, "lat", north)
    down = lax.ppermute(down, "lat", south)

    other = lax.ppermute(send, both, swap)
    chunks = small_kernel(
        pack_chunks,
        shape((n_x * n_yz, 16, 128), F32),
        keep,
        other,
        scratch=[pltpu.VMEM(keep.shape, F32)],
    )
    chunks = exchange(chunks.astype(jnp.float16), over_chips)

    up = up.reshape(RADIUS, across, 2 * width).astype(F32)
    down = down.reshape(RADIUS, across, 2 * width).astype(F32)
    rest = rows - RADIUS
    centre = centre.reshape(rows, across, 2 * width)
    centre = centre + jnp.pad(up, ((rest, 0), (0, 0), (0, 0))) + jnp.pad(down, ((0, rest), (0, 0), (0, 0)))
    to_east = centre[:, cols : cols + EDGE].astype(BF16)
    to_west = centre[:, cols + EDGE :].astype(BF16)
    from_west = lax.ppermute(to_east, "lon", east)
    from_east = lax.ppermute(to_west, "lon", west)
    chunks, from_west, from_east = lax.optimization_barrier((chunks, from_west, from_east))

    own = small_kernel(
        functools.partial(finish_chunk, grad_scale),
        shape((n_yz, 16, 128), BF16),
        chunks.astype(F32),
    )
    own = exchange(own, over_yz)

    rest = cols - EDGE
    owned = (
        centre[:, :cols]
        + jnp.pad(from_west.astype(F32), ((0, 0), (0, rest), (0, 0)))
        + jnp.pad(from_east.astype(F32), ((0, 0), (rest, 0), (0, 0)))
    )
    d_projected = jnp.concatenate([dq, owned.reshape(tokens, 2 * width).astype(BF16)], axis=1)
    grad_frame = (d_mid + nt(d_projected, weight_qkv)).astype(BF16)

    mine = small_kernel(join_chunks, shape((n_x, 784, 128), BF16), own)
    mine = exchange(mine, over_x)
    theirs = lax.ppermute(mine, both, swap)
    gradients = small_kernel(
        unpack,
        [
            shape((width, 3 * width), BF16),
            shape((width, width), BF16),
            shape((width, ff), BF16),
            shape((ff, width), BF16),
            shape((1, width), F32),
            shape((1, width), F32),
        ],
        where,
        mine,
        theirs,
    )
    gain_sums = [g.reshape(width) for g in gradients[4:]]
    return (
        block_out.reshape(rows, cols, width),
        grad_frame.reshape(rows, cols, width),
        *gradients[:4],
        *gain_sums,
    )


def solution(mesh):
    return jax.shard_map(
        on_device,
        mesh=mesh,
        in_specs=(P("lat", "lon", None), P(), P(), P(), P(), P(), P(), P("lat", "lon", None)),
        out_specs=(P("lat", "lon", None), P("lat", "lon", None), P(), P(), P(), P(), P(), P()),
        check_vma=False,
    )
```
